128 devices in a mesh: slab: 32 (over y, z, x_lo), beam: 4 (over x_hi, core).
Axes of the slice: x: 4 (x_hi: 2, x_lo: 2; x = x_hi * 2 + x_lo), y: 4, z: 4, core: 2. Of those that a mesh axis runs over, the one named last changes fastest.
Arguments:
- traces: bfloat16 [2048, 128, 1024], P(('slab', 'beam')), may hold values from -6 to 6
- shot_window: int32 [2048], P(('slab', 'beam')), may hold values from 0 to 15, as said below
- trace_slot: int32 [2048, 128], P(('slab', 'beam')), may hold values from 0 to 63
- ray_phase: bfloat16 [256, 1024], replicated, may hold values from -0.1875 to 0.1875
- ray_index: int32 [16, 768], P('beam', 'slab'), may hold values from 0 to 255
- beam_basis: bfloat16 [2, 1024, 8192], P(None, 'beam'), may hold values from -0.125 to 0.125
Outputs:
- image: float32 [768, 8192], P('slab', 'beam')
The draws below stay inside these ranges and needn't reach their ends.
Inputs may be any that keep to these rules, and one draw needn't show every extreme that they name: `shot_window`: within each aligned block of 16 shots (the shots of one device), for every beam owner b exactly 4 shots name a window w with w // 4 = b.
All inputs are finite; a program needn't handle non-finite values.
Results may differ from the reference program's by a relative error of at most 0.0041.
Values may be sent and summed in bfloat16 or wider, within the bound.
No kernel may reach another device: no remote copies, remote signals or barrier semaphores. Data moves between devices by JAX's collectives and lax.ppermute only.
A program may use at most 64 MiB of HBM per device.

```python
import math
import jax
import jax.numpy as jnp
from jax import lax

NF = 512
P_SIZE = 64
K = 64
WIN_OWN = 4
RAYS = 256
TPS = 128
SH_DEV = 16
LAT = 8192
WINDOWS = 16
SHOTS = 2048
NZ = 768


def draw_shot_window(key, part):
    owner_count = WINDOWS // WIN_OWN
    device_count = SHOTS // SH_DEV
    owner_pattern = jnp.tile(jnp.arange(owner_count, dtype=jnp.int32), SH_DEV // owner_count)
    key_list = jax.random.split(jax.random.fold_in(key, 7), device_count)
    shuffled = jax.vmap(lambda single_key: jax.random.permutation(single_key, owner_pattern))(key_list)
    within = jax.random.randint(jax.random.fold_in(key, 11), (device_count, SH_DEV), 0, WIN_OWN)
    return (shuffled * WIN_OWN + within).reshape(SHOTS).astype(jnp.int32)


def set_ends(array, own_key, least, largest):
    longest = array.shape.index(max(array.shape))
    spots = []
    for shift in (0, 1):
        where = [jax.random.randint(jax.random.fold_in(own_key, axis), (), 0, length) for axis, length in enumerate(array.shape)]
        where[longest] = (where[longest] + shift) % array.shape[longest]
        spots.append(tuple(where))
    return array.at[spots[0]].set(least).at[spots[1]].set(largest)


def block_scale(stream_key, shape, cuts, least, high):
    level = 1.0
    for position, blocks in cuts:
        steps = jax.random.uniform(jax.random.fold_in(jax.random.fold_in(stream_key, 6), position), (blocks,), jnp.float32, least / len(cuts), high / len(cuts))
        level = level * jnp.repeat(jnp.exp(steps), shape[position] // blocks).reshape((-1,) + (1,) * (len(shape) - 1 - position))
    return level


def normal_values(key, shape, width, limit, cuts=(), kind=jnp.bfloat16):
    gain = block_scale(key, shape, cuts, -0.22, 0.18) if cuts else 1.0
    result = jax.random.normal(key, shape, jnp.float32) * width * gain
    return jnp.minimum(jnp.maximum(result, -limit), limit).astype(kind)


def setup_inputs(seed: int = 0) -> dict:
    arg_keys = jax.random.split(jax.random.key(seed), 7)
    return {
        "traces": normal_values(arg_keys[0], (SHOTS, TPS, 2 * NF), 1.0, 6.0, ((0, 128),)),
        "shot_window": draw_shot_window(jax.random.fold_in(arg_keys[6], 71), 0),
        "trace_slot": set_ends(jax.random.randint(arg_keys[2], (SHOTS, TPS), 0, K), jax.random.fold_in(arg_keys[2], 1), 0, K - 1).astype(jnp.int32),
        "ray_phase": normal_values(arg_keys[3], (RAYS, 2 * NF), (2 * NF) ** -0.5, 0.1875),
        "ray_index": set_ends(jax.random.randint(arg_keys[4], (WINDOWS, NZ), 0, RAYS), jax.random.fold_in(arg_keys[4], 1), 0, RAYS - 1).astype(jnp.int32),
        "beam_basis": normal_values(arg_keys[5], (2, WINDOWS * P_SIZE, LAT), (2 * WINDOWS * P_SIZE) ** -0.5, 0.125, ((1, 4),)),
    }


def slant_tables():
    phase_steps = (jnp.arange(P_SIZE, dtype=jnp.int32)[:, None] * jnp.arange(K, dtype=jnp.int32)[None, :]) % K
    angles = phase_steps.astype(jnp.float32) * jnp.float32(2.0 * math.pi / K)
    return jnp.cos(angles), jnp.sin(angles)


def slant_stack(binned, cosine_table, sine_table):
    freq_count = binned.shape[-1] // 2
    real_part = binned[..., :freq_count]
    imag_part = binned[..., freq_count:]
    high = lax.Precision.HIGHEST
    panel_re = jnp.einsum("ps,wsf->wpf", cosine_table, real_part, precision=high) + jnp.einsum("ps,wsf->wpf", sine_table, imag_part, precision=high)
    panel_im = jnp.einsum("ps,wsf->wpf", cosine_table, imag_part, precision=high) - jnp.einsum("ps,wsf->wpf", sine_table, real_part, precision=high)
    return jnp.concatenate([panel_re, panel_im], axis=-1)


def reference(traces, shot_window, trace_slot, ray_phase, ray_index, beam_basis):
    block_count = SHOTS // SH_DEV
    trace_blocks = traces.reshape(block_count, SH_DEV * TPS, 2 * NF)
    labels = jnp.repeat(shot_window, TPS) * K + trace_slot.reshape(-1)
    label_blocks = labels.astype(jnp.int32).reshape(block_count, SH_DEV * TPS)

    def accumulate(running, pieces):
        samples, block_labels = pieces
        added = jax.ops.segment_sum(samples.astype(jnp.float32), block_labels, num_segments=WINDOWS * K)
        return running + added, None

    binned, _ = lax.scan(accumulate, jnp.zeros((WINDOWS * K, 2 * NF), jnp.float32), (trace_blocks, label_blocks))
    binned = binned.reshape(WINDOWS, K, 2 * NF)
    cosine_table, sine_table = slant_tables()
    stack_scale = jnp.float32((SHOTS * TPS / WINDOWS) ** -0.5)
    beam_panel = (slant_stack(binned, cosine_table, sine_table) * stack_scale).astype(jnp.bfloat16)
    rays = ray_phase[ray_index]
    panel_re = beam_panel[..., :NF]
    panel_im = beam_panel[..., NF:]
    left_re = jnp.concatenate([panel_re, -panel_im], axis=-1).astype(jnp.float32)
    left_im = jnp.concatenate([panel_im, panel_re], axis=-1).astype(jnp.float32)
    rays_wide = rays.astype(jnp.float32)
    wave_re = jnp.einsum("wzf,wpf->zwp", rays_wide, left_re).astype(jnp.bfloat16)
    wave_im = jnp.einsum("wzf,wpf->zwp", rays_wide, left_im).astype(jnp.bfloat16)
    mixture = jnp.concatenate([wave_re.reshape(NZ, WINDOWS * P_SIZE), -wave_im.reshape(NZ, WINDOWS * P_SIZE)], axis=1)
    basis_rows = beam_basis.reshape(2 * WINDOWS * P_SIZE, LAT)
    return jnp.dot(mixture, basis_rows, preferred_element_type=jnp.float32)
```

```python
import functools
import math

import jax
import jax.numpy as jnp
import numpy as np
from jax import lax
from jax.experimental import pallas as pl
from jax.experimental.pallas import tpu as pltpu
from jax.sharding import PartitionSpec as P

P_SIZE = 64
K = 64
WIN_OWN = 4
AXES = ("slab", "beam")
BF16 = jnp.bfloat16
F32 = jnp.float32


def slant_table(scale):
    steps = np.arange(P_SIZE)[:, None] * np.arange(K)[None, :] % K
    angles = steps * (2.0 * math.pi / K)
    c, d = np.cos(angles) * scale, np.sin(angles) * scale
    full = np.stack([np.concatenate([c, d]), np.concatenate([d, -c])])
    full = full.astype(np.float32)
    high = full.astype(BF16)
    low = (full - high.astype(np.float32)).astype(BF16)
    table = np.concatenate([high[0], low[0], high[1], low[1]], axis=0)
    return np.pad(table, ((0, 0), (0, 128 - K)))


def split(value):
    high = value.astype(BF16)
    return high, (value - high.astype(F32)).astype(BF16)


def ray_weights(ray_ref, weight_ref):
    rays, doubled = ray_ref.shape
    half = doubled // 2
    weight_ref[:rays, :half] = ray_ref[:, :half]
    weight_ref[:rays, half:] = -ray_ref[:, half:]
    weight_ref[rays:, :half] = ray_ref[:, half:]
    weight_ref[rays:, half:] = ray_ref[:, :half]


NT = (((1,), (1,)), ((), ()))


def stack_kernel(group, window_ref, slot_ref, table_ref, ray_ref, trace_ref, out_ref, weight_ref, acc_ref):
    step = pl.program_id(0)
    rays = ray_ref.shape[0]
    per_shot = trace_ref.shape[1]

    @pl.when(step == 0)
    def _():
        ray_weights(ray_ref, weight_ref)
        acc_ref[...] = jnp.zeros_like(acc_ref)

    samples = trace_ref[...].reshape(group * per_shot, trace_ref.shape[2])
    value = lax.dot_general(samples, weight_ref[...], NT, preferred_element_type=F32)
    high, low = split(value)
    slot_rows = lax.broadcasted_iota(jnp.int32, (128, per_shot), 0)
    for j in range(group):
        shot = step * group + j
        slots = slot_ref[pl.ds(shot, 1), :]
        pick = (slot_rows == slots).astype(F32).astype(BF16)
        factors = jnp.dot(table_ref[...], pick, preferred_element_type=F32).astype(BF16)
        factors = jnp.concatenate([factors[:256], factors[256:]], axis=1)
        rows = slice(j * per_shot, (j + 1) * per_shot)
        right_high = jnp.concatenate([high[rows, :rays], high[rows, rays:]], axis=0)
        right_low = jnp.concatenate([low[rows, :rays], low[rows, rays:]], axis=0)
        one = jnp.dot(factors, right_high, preferred_element_type=F32)
        two = jnp.dot(factors[:128], right_low, preferred_element_type=F32)
        window = window_ref[shot]
        acc_ref[window] += one[:128] + one[128:] + two

    @pl.when(step == pl.num_programs(0) - 1)
    def _():
        for b in range(4):
            for wl in range(WIN_OWN):
                for h in range(2):
                    block = acc_ref[b * WIN_OWN + wl, h * 64 : (h + 1) * 64, :].astype(BF16)
                    first = h * 16 + wl * 4
                    out_ref[first : first + 4, b] = block.reshape(4, 16, rays)


def stack(window, slots, table, ray_phase, traces):
    shots, per_shot, doubled = traces.shape
    rays = ray_phase.shape[0]
    group = 4
    whole = lambda shape: pl.BlockSpec(shape, lambda i, w: (0,) * len(shape))
    return pl.pallas_call(
        functools.partial(stack_kernel, group),
        out_shape=jax.ShapeDtypeStruct((32, 4, 16, rays), BF16),
        grid_spec=pltpu.PrefetchScalarGridSpec(
            num_scalar_prefetch=1,
            grid=(shots // group,),
            in_specs=[
                whole(slots.shape),
                whole(table.shape),
                whole(ray_phase.shape),
                pl.BlockSpec((group, per_shot, doubled), lambda i, w: (i, 0, 0)),
            ],
            out_specs=whole((32, 4, 16, rays)),
            scratch_shapes=[
                pltpu.VMEM((2 * rays, doubled), BF16),
                pltpu.VMEM((16, 2 * P_SIZE, rays), F32),
            ],
        ),
        compiler_params=pltpu.CompilerParams(vmem_limit_bytes=32 << 20),
        name="stack",
    )(window, slots, table, ray_phase, traces)


def image_kernel(index_ref, ray_ref, basis_ref, out_ref, left_ref):
    @pl.when(pl.program_id(0) == 0)
    def _():
        rays = ray_ref.shape[-1]
        depths = index_ref.shape[0] // WIN_OWN
        lanes = lax.broadcasted_iota(jnp.int32, (WIN_OWN * depths, rays), 1)
        index = jnp.concatenate([index_ref[...], index_ref[...]], axis=1)
        pick = (lanes == index).astype(F32).astype(BF16)
        group = lax.broadcasted_iota(jnp.int32, (depths, 512), 1) // P_SIZE % WIN_OWN
        for part in range(2):
            table = ray_ref[:, part].reshape(512, rays)
            waves = lax.dot_general(pick, table, NT, preferred_element_type=F32)
            wave = waves[:depths]
            for wl in range(1, WIN_OWN):
                wave = jnp.where(group == wl, waves[wl * depths : (wl + 1) * depths], wave)
            left_ref[part * depths : (part + 1) * depths, :] = wave

    depths = out_ref.shape[1]
    basis = basis_ref[...].reshape(512, basis_ref.shape[2])
    terms = jnp.dot(left_ref[...].astype(BF16), basis, preferred_element_type=F32)
    out_ref[0] = (terms[:depths] + terms[depths:]).astype(BF16)


def image(index, rays, basis):
    depths = index.shape[0] // WIN_OWN
    laterals = basis.shape[2]
    tile = 1024
    per = laterals // 4 // tile
    whole = lambda shape: pl.BlockSpec(shape, lambda i: (0,) * len(shape))
    return pl.pallas_call(
        image_kernel,
        out_shape=jax.ShapeDtypeStruct((4, depths, laterals // 4), BF16),
        grid=(laterals // tile,),
        in_specs=[
            whole(index.shape),
            whole(rays.shape),
            pl.BlockSpec((2, 256, tile), lambda i: (0, 0, i)),
        ],
        out_specs=pl.BlockSpec((1, depths, tile), lambda i: (i // per, 0, i % per)),
        scratch_shapes=[pltpu.VMEM((2 * depths, 512), F32)],
        compiler_params=pltpu.CompilerParams(vmem_limit_bytes=32 << 20),
        name="image",
    )(index, rays, basis)


def body(traces, shot_window, trace_slot, ray_phase, ray_index, beam_basis):
    shots, per_shot, doubled = traces.shape
    rays = ray_phase.shape[0]
    depths = ray_index.shape[1]
    devices = lax.axis_size("slab") * lax.axis_size("beam")
    scale = (shots * devices * per_shot / (WIN_OWN * lax.axis_size("beam"))) ** -0.5
    index = jnp.broadcast_to(ray_index.reshape(WIN_OWN * depths, 1), (WIN_OWN * depths, 128))
    part = stack(shot_window, trace_slot, slant_table(scale), ray_phase, traces)
    arrived = lax.all_to_all(part.reshape(devices, 16, rays), AXES, 0, 0, tiled=True)
    mine = jnp.sum(arrived.astype(F32), axis=0)
    pair = jnp.stack(split(mine))
    sent = jnp.broadcast_to(pair[None], (32, 2, 16, rays))
    table = lax.all_to_all(sent, "slab", 0, 0, tiled=True)
    terms = image(index, table, beam_basis)
    arrived = lax.all_to_all(terms, "beam", 0, 0, tiled=True)
    return jnp.sum(arrived.astype(F32), axis=0)


def solution(mesh):
    in_specs = (
        P(("slab", "beam"), None, None),
        P(("slab", "beam")),
        P(("slab", "beam"), None),
        P(),
        P("beam", "slab"),
        P(None, "beam", None),
    )
    return jax.shard_map(
        body, mesh=mesh, in_specs=in_specs, out_specs=P("slab", "beam"), check_vma=False
    )
```

```python
import functools
import math

import jax
import jax.numpy as jnp
import numpy as np
from jax import lax
from jax.experimental import pallas as pl
from jax.experimental.pallas import tpu as pltpu
from jax.sharding import PartitionSpec as P


P_SIZE = 64
K = 64
WIN_OWN = 4
AXES = ("slab", "beam")
BF16 = jnp.bfloat16
F32 = jnp.float32
NT = (((1,), (1,)), ((), ()))
HBM = pl.BlockSpec(memory_space=pltpu.HBM)
VMEM = pl.BlockSpec(memory_space=pltpu.VMEM)


def slant_table(scale):
    steps = np.arange(P_SIZE)[:, None] * np.arange(K)[None, :] % K
    angles = steps * (2.0 * math.pi / K)
    full = (np.concatenate([np.cos(angles), np.sin(angles)]) * scale).astype(np.float32)
    high = full.astype(BF16)
    low = (full - high.astype(np.float32)).astype(BF16)
    return np.pad(np.concatenate([high, low]), ((0, 0), (0, 128 - K)))


def split(value):
    high = value.astype(BF16)
    return high, (value - high.astype(F32)).astype(BF16)


def beam_position():
    position = lax.axis_index("beam")
    return lax.div(position, 2), lax.rem(position, 2)


def stack_kernel(
    group, window_hbm, slot_hbm, table_hbm, ray_hbm, trace_hbm, mine_ref, other_ref,
    buffer, window_ref, slot_ref, table_ref, ray_ref, weight_ref, acc_ref, sems, trace_sems,
):
    rays, doubled = ray_ref.shape
    half = doubled // 2
    shots, per_shot, _ = trace_hbm.shape
    pairs = ((window_hbm, window_ref), (ray_hbm, ray_ref), (slot_hbm, slot_ref), (table_hbm, table_ref))
    small = [pltpu.make_async_copy(a, b, sems.at[i]) for i, (a, b) in enumerate(pairs)]
    loads = []
    for g in range(shots // group):
        part = pl.ds(g * group, group)
        loads.append(pltpu.make_async_copy(trace_hbm.at[part], buffer.at[part], trace_sems.at[g]))
    for copy in small + loads:
        copy.start()
    _, core = beam_position()
    acc_ref[...] = jnp.zeros_like(acc_ref)
    small[1].wait()
    weight_ref[:rays, :half] = ray_ref[:, :half]
    weight_ref[:rays, half:] = -ray_ref[:, half:]
    weight_ref[rays:, :half] = ray_ref[:, half:]
    weight_ref[rays:, half:] = ray_ref[:, :half]
    for copy in (small[0], small[2], small[3]):
        copy.wait()
    slot_rows = lax.broadcasted_iota(jnp.int32, (128, per_shot), 0)
    for g in range(shots // group):
        first = g * group
        factors = []
        for j in range(0, group, 2):
            picks = []
            for shot in (first + j, first + j + 1):
                slots = slot_ref[shot : shot + 1, :]
                picks.append((slot_rows == slots).astype(F32).astype(BF16))
            both = jnp.dot(
                table_ref[...], jnp.concatenate(picks, axis=1), preferred_element_type=F32
            ).astype(BF16)
            for i in range(2):
                left = both[:, i * per_shot : (i + 1) * per_shot]
                right = jnp.concatenate(
                    [left[64:128], -left[:64], left[192:], -left[128:192]], axis=0
                )
                factors.append(jnp.concatenate([left, right], axis=1))
        loads[g].wait()
        samples = buffer[first : first + group].reshape(group * per_shot, doubled)
        value = lax.dot_general(samples, weight_ref[...], NT, preferred_element_type=F32)
        high, low = split(value)
        for j in range(group):
            rows = slice(j * per_shot, (j + 1) * per_shot)
            right_high = jnp.concatenate([high[rows, :rays], high[rows, rays:]], axis=0)
            right_low = jnp.concatenate([low[rows, :rays], low[rows, rays:]], axis=0)
            one = jnp.dot(factors[j], right_high, preferred_element_type=F32)
            two = jnp.dot(factors[j][:128], right_low, preferred_element_type=F32)
            window = window_ref[first + j]
            away = ((window >> 2) & 1) ^ core
            acc_ref[away * 8 + (window >> 3) * 4 + (window & 3)] += one[:128] + one[128:] + two
    for side in range(2):
        for wl in range(WIN_OWN):
            for h in range(2):
                at = h * 16 + wl * 4
                rows = slice(h * 64, (h + 1) * 64)
                block = acc_ref[side * 4 + wl, rows]
                mine_ref[at : at + 4, side] = block.reshape(4, 16, rays)
                block = acc_ref[8 + side * 4 + wl, rows].astype(other_ref.dtype)
                other_ref[at : at + 4, side] = block.reshape(4, 16, rays)


def stack(window, slots, table, ray_phase, traces):
    shots, _, doubled = traces.shape
    rays = ray_phase.shape[0]
    group = 4
    return pl.pallas_call(
        functools.partial(stack_kernel, group),
        out_shape=(
            jax.ShapeDtypeStruct((32, 2, 16, rays), F32),
            jax.ShapeDtypeStruct((32, 2, 16, rays), BF16),
        ),
        in_specs=[HBM] * 5,
        out_specs=(VMEM, VMEM),
        scratch_shapes=[
            pltpu.VMEM(traces.shape, BF16),
            pltpu.SMEM(window.shape, jnp.int32),
            pltpu.VMEM(slots.shape, jnp.int32),
            pltpu.VMEM(table.shape, BF16),
            pltpu.VMEM(ray_phase.shape, BF16),
            pltpu.VMEM((2 * rays, doubled), BF16),
            pltpu.VMEM((16, 2 * P_SIZE, rays), F32),
            pltpu.SemaphoreType.DMA((4,)),
            pltpu.SemaphoreType.DMA((shots // group,)),
        ],
        compiler_params=pltpu.CompilerParams(vmem_limit_bytes=STACK_VMEM),
        name="stack",
    )(window, slots, table, ray_phase, traces)


STACK_VMEM = 61 << 20
IMAGE_VMEM = 57 << 20


def spread_kernel(arrived_ref, out_ref):
    total = jnp.sum(arrived_ref[...].astype(F32), axis=0).astype(out_ref.dtype)
    for i in range(out_ref.shape[0]):
        out_ref[i] = total


def spread(arrived):
    return pl.pallas_call(
        spread_kernel,
        out_shape=jax.ShapeDtypeStruct((32,) + arrived.shape[1:], BF16),
        in_specs=[VMEM],
        out_specs=VMEM,
        name="spread",
    )(arrived)


def select(index_ref, table_ref, lane_ref):
    rays = table_ref.shape[-1]
    depths = index_ref.shape[1]
    lane_ref[:WIN_OWN, :depths] = index_ref[...]
    spread_out = lane_ref[...]
    lane = lax.broadcasted_iota(jnp.int32, (1, 128), 1)
    index = jnp.zeros((1, 128), jnp.int32)
    for wl in range(WIN_OWN):
        moved = pltpu.roll(spread_out, wl * depths, 1)[wl : wl + 1]
        here = (lane >= wl * depths) & (lane < (wl + 1) * depths)
        index = jnp.where(here, moved, index)
    rows = lax.broadcasted_iota(jnp.int32, (rays, 128), 0)
    pick = jnp.transpose((rows == index).astype(F32)).astype(BF16)
    group = lax.broadcasted_iota(jnp.int32, (depths, 512), 1) // P_SIZE % WIN_OWN
    table = table_ref[...].reshape(512, rays)
    waves = lax.dot_general(pick, table, NT, preferred_element_type=F32)
    wave = waves[:depths]
    for wl in range(1, WIN_OWN):
        wave = jnp.where(group == wl, waves[wl * depths : (wl + 1) * depths], wave)
    return wave.astype(BF16)


PIECES = 4


def basis_loads(far, other, basis_hbm, basis_ref, sems):
    side, core = beam_position()
    chunk = (1 - side if far else side) * 2 + (1 - core if other else core)
    width = basis_ref.shape[2] // PIECES
    loads = []
    for i in range(PIECES):
        source = pl.ds(pl.multiple_of(chunk * basis_ref.shape[2] + i * width, width), width)
        target = pl.ds(i * width, width)
        loads.append(
            pltpu.make_async_copy(
                basis_hbm.at[:, :, source], basis_ref.at[:, :, target], sems.at[i]
            )
        )
        loads[-1].start()
    return loads


def multiply(wave, loads, basis_ref, out_ref):
    width = basis_ref.shape[2] // PIECES
    for i, load in enumerate(loads):
        load.wait()
        columns = slice(i * width, (i + 1) * width)
        basis = basis_ref[:, :, columns].reshape(512, width)
        out_ref[:, columns] = jnp.dot(wave, basis, preferred_element_type=F32)


def first_kernel(index_ref, table_ref, basis_hbm, out_ref, wave_ref, basis_ref, sems, lane_ref):
    loads = basis_loads(True, True, basis_hbm, basis_ref, sems)
    wave_ref[...] = select(index_ref, table_ref, lane_ref)
    multiply(wave_ref[...], loads, basis_ref, out_ref)


def later_kernel(far, other, wave_ref, basis_hbm, out_ref, basis_ref, sems):
    loads = basis_loads(far, other, basis_hbm, basis_ref, sems)
    multiply(wave_ref[...], loads, basis_ref, out_ref)


def image_call(kernel, depths, laterals, basis, wave_out, *operands):
    shape = jax.ShapeDtypeStruct((depths, laterals), F32)
    wave = jax.ShapeDtypeStruct((depths, 512), BF16)
    return pl.pallas_call(
        kernel,
        out_shape=(shape, wave) if wave_out else shape,
        in_specs=[VMEM] * len(operands) + [HBM],
        out_specs=(VMEM, VMEM) if wave_out else VMEM,
        scratch_shapes=[
            pltpu.VMEM((2, 256, laterals), BF16),
            pltpu.SemaphoreType.DMA((PIECES,)),
        ]
        + [pltpu.VMEM((8, 128), jnp.int32)] * wave_out,
        compiler_params=pltpu.CompilerParams(vmem_limit_bytes=IMAGE_VMEM),
        cost_estimate=pl.CostEstimate(
            flops=2 * depths * 512 * laterals, bytes_accessed=1024 * laterals, transcendentals=0
        ),
    )(*operands, basis)


def body(traces, shot_window, trace_slot, ray_phase, ray_index, beam_basis):
    shots, per_shot, _ = traces.shape
    rays = ray_phase.shape[0]
    depths = ray_index.shape[1]
    slabs, beams = lax.axis_size("slab"), lax.axis_size("beam")
    devices = slabs * beams
    chunk = beam_basis.shape[2] // beams
    scale = (shots * devices * per_shot / (WIN_OWN * beams)) ** -0.5
    partner = [(i, i ^ 1) for i in range(devices)]
    distant = [(i, i ^ 2) for i in range(devices)]
    same_core = [list(range(core, devices, 2)) for core in range(2)]

    mine, other = stack(shot_window, trace_slot, slant_table(scale), ray_phase, traces)
    other = lax.ppermute(other, AXES, partner)
    both = (mine + other.astype(F32)).astype(BF16).reshape(2 * slabs, 16, rays)
    arrived = lax.all_to_all(both, AXES, 0, 0, axis_index_groups=same_core, tiled=True)
    table = lax.all_to_all(spread(arrived), "slab", 0, 0, tiled=True)

    far_other, wave = image_call(first_kernel, depths, chunk, beam_basis, True, ray_index, table)
    call = lambda far, other, wave: image_call(
        functools.partial(later_kernel, far, other), depths, chunk, beam_basis, False, wave
    )
    far_other = lax.ppermute(far_other, AXES, partner)
    far_mine = call(True, False, wave)
    far = (far_mine + far_other).astype(BF16)
    far = lax.ppermute(far, AXES, distant)
    near_other = call(False, True, wave)
    near_other = lax.ppermute(near_other, AXES, partner)
    near_mine = call(False, False, wave)
    return near_mine + near_other + far.astype(F32)


def solution(mesh):
    in_specs = (
        P(("slab", "beam"), None, None),
        P(("slab", "beam")),
        P(("slab", "beam"), None),
        P(),
        P("beam", "slab"),
        P(None, "beam", None),
    )
    return jax.shard_map(
        body, mesh=mesh, in_specs=in_specs, out_specs=P("slab", "beam"), check_vma=False
    )
```

```python
import functools
import math

import jax
import jax.numpy as jnp
import numpy as np
from jax import lax
from jax.experimental import pallas as pl
from jax.experimental.pallas import tpu as pltpu
from jax.sharding import PartitionSpec as P


P_SIZE = 64
K = 64
WIN_OWN = 4
AXES = ("slab", "beam")
BF16 = jnp.bfloat16
F32 = jnp.float32
NT = (((1,), (1,)), ((), ()))
HBM = pl.BlockSpec(memory_space=pltpu.HBM)
VMEM = pl.BlockSpec(memory_space=pltpu.VMEM)


def slant_table(scale):
    steps = np.arange(P_SIZE)[:, None] * np.arange(K)[None, :] % K
    angles = steps * (2.0 * math.pi / K)
    full = (np.concatenate([np.cos(angles), np.sin(angles)]) * scale).astype(np.float32)
    high = full.astype(BF16)
    low = (full - high.astype(np.float32)).astype(BF16)
    return np.pad(np.concatenate([high, low]), ((0, 0), (0, 128 - K)))


def split(value):
    high = value.astype(BF16)
    return high, (value - high.astype(F32)).astype(BF16)


def beam_position():
    position = lax.axis_index("beam")
    return lax.div(position, 2), lax.rem(position, 2)


def stack_kernel(
    group, window_hbm, slot_hbm, table_hbm, ray_hbm, trace_hbm, mine_ref, other_ref,
    buffer, window_ref, slot_ref, table_ref, ray_ref, weight_ref, acc_ref, sems, trace_sems,
):
    rays, doubled = ray_ref.shape
    half = doubled // 2
    shots, per_shot, _ = trace_hbm.shape
    pairs = ((window_hbm, window_ref), (ray_hbm, ray_ref), (slot_hbm, slot_ref), (table_hbm, table_ref))
    small = [pltpu.make_async_copy(a, b, sems.at[i]) for i, (a, b) in enumerate(pairs)]
    loads = []
    for g in range(shots // group):
        part = pl.ds(g * group, group)
        loads.append(pltpu.make_async_copy(trace_hbm.at[part], buffer.at[part], trace_sems.at[g]))
    for copy in small + loads:
        copy.start()
    _, core = beam_position()
    acc_ref[...] = jnp.zeros_like(acc_ref)
    small[1].wait()
    weight_ref[:rays, :half] = ray_ref[:, :half]
    weight_ref[:rays, half:] = -ray_ref[:, half:]
    weight_ref[rays:, :half] = ray_ref[:, half:]
    weight_ref[rays:, half:] = ray_ref[:, :half]
    for copy in (small[0], small[2], small[3]):
        copy.wait()
    slot_rows = lax.broadcasted_iota(jnp.int32, (128, per_shot), 0)
    for g in range(shots // group):
        first = g * group
        factors = []
        for j in range(0, group, 2):
            picks = []
            for shot in (first + j, first + j + 1):
                slots = slot_ref[shot : shot + 1, :]
                picks.append((slot_rows == slots).astype(F32).astype(BF16))
            both = jnp.dot(
                table_ref[...], jnp.concatenate(picks, axis=1), preferred_element_type=F32
            ).astype(BF16)
            for i in range(2):
                left = both[:, i * per_shot : (i + 1) * per_shot]
                right = jnp.concatenate(
                    [left[64:128], -left[:64], left[192:], -left[128:192]], axis=0
                )
                factors.append(jnp.concatenate([left, right], axis=1))
        loads[g].wait()
        samples = buffer[first : first + group].reshape(group * per_shot, doubled)
        value = lax.dot_general(samples, weight_ref[...], NT, preferred_element_type=F32)
        high, low = split(value)
        for j in range(group):
            rows = slice(j * per_shot, (j + 1) * per_shot)
            right_high = jnp.concatenate([high[rows, :rays], high[rows, rays:]], axis=0)
            right_low = jnp.concatenate([low[rows, :rays], low[rows, rays:]], axis=0)
            one = jnp.dot(factors[j], right_high, preferred_element_type=F32)
            two = jnp.dot(factors[j][:128], right_low, preferred_element_type=F32)
            window = window_ref[first + j]
            away = ((window >> 2) & 1) ^ core
            acc_ref[away * 8 + (window >> 3) * 4 + (window & 3)] += one[:128] + one[128:] + two
    for side in range(2):
        for wl in range(WIN_OWN):
            for h in range(2):
                at = h * 16 + wl * 4
                rows = slice(h * 64, (h + 1) * 64)
                block = acc_ref[side * 4 + wl, rows]
                mine_ref[at : at + 4, side] = block.reshape(4, 16, rays)
                block = acc_ref[8 + side * 4 + wl, rows].astype(other_ref.dtype)
                other_ref[at : at + 4, side] = block.reshape(4, 16, rays)


def stack(window, slots, table, ray_phase, traces):
    shots, _, doubled = traces.shape
    rays = ray_phase.shape[0]
    group = 4
    return pl.pallas_call(
        functools.partial(stack_kernel, group),
        out_shape=(
            jax.ShapeDtypeStruct((32, 2, 16, rays), F32),
            jax.ShapeDtypeStruct((32, 2, 16, rays), BF16),
        ),
        in_specs=[HBM] * 5,
        out_specs=(VMEM, VMEM),
        scratch_shapes=[
            pltpu.VMEM(traces.shape, BF16),
            pltpu.SMEM(window.shape, jnp.int32),
            pltpu.VMEM(slots.shape, jnp.int32),
            pltpu.VMEM(table.shape, BF16),
            pltpu.VMEM(ray_phase.shape, BF16),
            pltpu.VMEM((2 * rays, doubled), BF16),
            pltpu.VMEM((16, 2 * P_SIZE, rays), F32),
            pltpu.SemaphoreType.DMA((4,)),
            pltpu.SemaphoreType.DMA((shots // group,)),
        ],
        compiler_params=pltpu.CompilerParams(vmem_limit_bytes=STACK_VMEM),
        name="stack",
    )(window, slots, table, ray_phase, traces)


STACK_VMEM = 54 << 20
IMAGE_VMEM = 12 << 20


def spread_kernel(arrived_ref, out_ref):
    total = jnp.sum(arrived_ref[...].astype(F32), axis=0).astype(out_ref.dtype)
    for i in range(out_ref.shape[0]):
        out_ref[i] = total


def spread(arrived):
    return pl.pallas_call(
        spread_kernel,
        out_shape=jax.ShapeDtypeStruct((32,) + arrived.shape[1:], BF16),
        in_specs=[VMEM],
        out_specs=VMEM,
        compiler_params=pltpu.CompilerParams(vmem_limit_bytes=8 << 20),
        name="spread",
    )(arrived)


def select(index_ref, table_ref, lane_ref):
    rays = table_ref.shape[-1]
    depths = index_ref.shape[1]
    lane_ref[:WIN_OWN, :depths] = index_ref[...]
    spread_out = lane_ref[...]
    lane = lax.broadcasted_iota(jnp.int32, (1, 128), 1)
    index = jnp.zeros((1, 128), jnp.int32)
    for wl in range(WIN_OWN):
        moved = pltpu.roll(spread_out, wl * depths, 1)[wl : wl + 1]
        here = (lane >= wl * depths) & (lane < (wl + 1) * depths)
        index = jnp.where(here, moved, index)
    rows = lax.broadcasted_iota(jnp.int32, (rays, 128), 0)
    pick = jnp.transpose((rows == index).astype(F32)).astype(BF16)
    group = lax.broadcasted_iota(jnp.int32, (depths, 512), 1) // P_SIZE % WIN_OWN
    table = table_ref[...].reshape(512, rays)
    waves = lax.dot_general(pick, table, NT, preferred_element_type=F32)
    wave = waves[:depths]
    for wl in range(1, WIN_OWN):
        wave = jnp.where(group == wl, waves[wl * depths : (wl + 1) * depths], wave)
    return wave.astype(BF16)


def multiply(far, other, wave, basis_ref, out_ref):
    side, core = beam_position()
    chunk = (1 - side if far else side) * 2 + (1 - core if other else core)
    laterals = out_ref.shape[1]
    width = 512
    for i in range(laterals // width):
        columns = pl.ds(pl.multiple_of(chunk * laterals + i * width, width), width)
        basis = basis_ref[:, :, columns].reshape(512, width)
        out_ref[:, i * width : (i + 1) * width] = jnp.dot(
            wave, basis, preferred_element_type=F32
        )


def first_kernel(index_ref, table_ref, basis_ref, out_ref, wave_ref, lane_ref):
    wave_ref[...] = select(index_ref, table_ref, lane_ref)
    multiply(True, True, wave_ref[...], basis_ref, out_ref)


def later_kernel(far, other, wave_ref, basis_ref, out_ref):
    multiply(far, other, wave_ref[...], basis_ref, out_ref)


def image_call(kernel, depths, laterals, basis, wave_out, *operands):
    shape = jax.ShapeDtypeStruct((depths, laterals), F32)
    wave = jax.ShapeDtypeStruct((depths, 512), BF16)
    return pl.pallas_call(
        kernel,
        out_shape=(shape, wave) if wave_out else shape,
        in_specs=[VMEM] * (len(operands) + 1),
        out_specs=(VMEM, VMEM) if wave_out else VMEM,
        scratch_shapes=[pltpu.VMEM((8, 128), jnp.int32)] * wave_out,
        compiler_params=pltpu.CompilerParams(vmem_limit_bytes=IMAGE_VMEM),
        cost_estimate=pl.CostEstimate(
            flops=2 * depths * 512 * laterals, bytes_accessed=1024 * laterals, transcendentals=0
        ),
    )(*operands, basis)


def body(traces, shot_window, trace_slot, ray_phase, ray_index, beam_basis):
    shots, per_shot, _ = traces.shape
    rays = ray_phase.shape[0]
    depths = ray_index.shape[1]
    slabs, beams = lax.axis_size("slab"), lax.axis_size("beam")
    devices = slabs * beams
    chunk = beam_basis.shape[2] // beams
    scale = (shots * devices * per_shot / (WIN_OWN * beams)) ** -0.5
    partner = [(i, i ^ 1) for i in range(devices)]
    distant = [(i, i ^ 2) for i in range(devices)]
    same_core = [list(range(core, devices, 2)) for core in range(2)]

    mine, other = stack(shot_window, trace_slot, slant_table(scale), ray_phase, traces)
    other = lax.ppermute(other, AXES, partner)
    both = (mine + other.astype(F32)).astype(BF16).reshape(2 * slabs, 16, rays)
    arrived = lax.all_to_all(both, AXES, 0, 0, axis_index_groups=same_core, tiled=True)
    table = lax.all_to_all(spread(arrived), "slab", 0, 0, tiled=True)

    far_other, wave = image_call(first_kernel, depths, chunk, beam_basis, True, ray_index, table)
    call = lambda far, other, wave: image_call(
        functools.partial(later_kernel, far, other), depths, chunk, beam_basis, False, wave
    )
    far_other = lax.ppermute(far_other, AXES, partner)
    far_mine = call(True, False, wave)
    far = (far_mine + far_other).astype(BF16)
    far = lax.ppermute(far, AXES, distant)
    near_other = call(False, True, wave)
    near_other = lax.ppermute(near_other, AXES, partner)
    near_mine = call(False, False, wave)
    return near_mine + near_other + far.astype(F32)


def solution(mesh):
    in_specs = (
        P(("slab", "beam"), None, None),
        P(("slab", "beam")),
        P(("slab", "beam"), None),
        P(),
        P("beam", "slab"),
        P(None, "beam", None),
    )
    return jax.shard_map(
        body, mesh=mesh, in_specs=in_specs, out_specs=P("slab", "beam"), check_vma=False
    )
```

```python
import functools
import math

import jax
import jax.numpy as jnp
import numpy as np
from jax import lax
from jax.experimental import pallas as pl
from jax.experimental.pallas import tpu as pltpu
from jax.sharding import PartitionSpec as P


P_SIZE = 64
K = 64
WIN_OWN = 4
AXES = ("slab", "beam")
BF16 = jnp.bfloat16
F32 = jnp.float32
NT = (((1,), (1,)), ((), ()))
HBM = pl.BlockSpec(memory_space=pltpu.HBM)
VMEM = pl.BlockSpec(memory_space=pltpu.VMEM)


def slant_table(scale):
    steps = np.arange(P_SIZE)[:, None] * np.arange(K)[None, :] % K
    angles = steps * (2.0 * math.pi / K)
    full = (np.concatenate([np.cos(angles), np.sin(angles)]) * scale).astype(np.float32)
    high = full.astype(BF16)
    low = (full - high.astype(np.float32)).astype(BF16)
    return np.pad(np.concatenate([high, low]), ((0, 0), (0, 128 - K)))


def split(value):
    high = value.astype(BF16)
    return high, (value - high.astype(F32)).astype(BF16)


def beam_position():
    position = lax.axis_index("beam")
    return lax.div(position, 2), lax.rem(position, 2)


def stack_kernel(
    group, window_hbm, slot_hbm, table_hbm, ray_hbm, trace_hbm, mine_ref, other_ref,
    buffer, window_ref, slot_ref, table_ref, ray_ref, weight_ref, factor_ref, high_ref, low_ref,
    acc_ref, sems, trace_sems,
):
    rays, doubled = ray_ref.shape
    half = doubled // 2
    shots, per_shot, _ = trace_hbm.shape
    groups = shots // group
    pairs = ((slot_hbm, slot_ref), (table_hbm, table_ref), (ray_hbm, ray_ref), (window_hbm, window_ref))
    small = [pltpu.make_async_copy(a, b, sems.at[i]) for i, (a, b) in enumerate(pairs)]
    loads = []
    for g in range(groups):
        part = pl.ds(g * group, group)
        loads.append(pltpu.make_async_copy(trace_hbm.at[part], buffer.at[part], trace_sems.at[g]))
    for copy in small + loads:
        copy.start()
    _, core = beam_position()
    acc_ref[...] = jnp.zeros_like(acc_ref)

    small[0].wait()
    small[1].wait()
    slot_rows = lax.broadcasted_iota(jnp.int32, (128, per_shot), 0)
    for first in range(0, shots, 2):
        picks = []
        for shot in (first, first + 1):
            slots = slot_ref[shot : shot + 1, :]
            picks.append((slot_rows == slots).astype(F32).astype(BF16))
        both = jnp.dot(
            table_ref[...], jnp.concatenate(picks, axis=1), preferred_element_type=F32
        ).astype(BF16)
        for i in range(2):
            left = both[:, i * per_shot : (i + 1) * per_shot]
            factor_ref[first + i, :, :per_shot] = left
            factor_ref[first + i, :, per_shot:] = jnp.concatenate(
                [left[64:128], -left[:64], left[192:], -left[128:192]], axis=0
            )
    small[2].wait()
    weight_ref[:rays, :half] = ray_ref[:, :half]
    weight_ref[:rays, half:] = -ray_ref[:, half:]
    weight_ref[rays:, :half] = ray_ref[:, half:]
    weight_ref[rays:, half:] = ray_ref[:, :half]
    small[3].wait()

    def slant(g):
        slot = g % 2
        for j in range(group):
            shot = g * group + j
            rows = slice(j * per_shot, (j + 1) * per_shot)
            right_high = jnp.concatenate(
                [high_ref[slot, rows, :rays], high_ref[slot, rows, rays:]], axis=0
            )
            right_low = jnp.concatenate(
                [low_ref[slot, rows, :rays], low_ref[slot, rows, rays:]], axis=0
            )
            one = jnp.dot(factor_ref[shot], right_high, preferred_element_type=F32)
            two = jnp.dot(factor_ref[shot, :128], right_low, preferred_element_type=F32)
            window = window_ref[shot]
            away = ((window >> 2) & 1) ^ core
            acc_ref[away * 8 + (window >> 3) * 4 + (window & 3)] += one[:128] + one[128:] + two

    for g in range(groups):
        if g < 2:
            for load in loads[g : 1 if g == 0 else groups]:
                load.wait()
        samples = buffer[g * group : (g + 1) * group].reshape(group * per_shot, doubled)
        value = lax.dot_general(samples, weight_ref[...], NT, preferred_element_type=F32)
        high_ref[g % 2], low_ref[g % 2] = split(value)
        if g > 0:
            slant(g - 1)
    slant(groups - 1)
    for side in range(2):
        for wl in range(WIN_OWN):
            for h in range(2):
                at = h * 16 + wl * 4
                rows = slice(h * 64, (h + 1) * 64)
                block = acc_ref[side * 4 + wl, rows]
                mine_ref[at : at + 4, side] = block.reshape(4, 16, rays)
                block = acc_ref[8 + side * 4 + wl, rows].astype(other_ref.dtype)
                other_ref[at : at + 4, side] = block.reshape(4, 16, rays)


def stack(*operands):
    window, slots, table, ray_phase, traces = operands
    shots, per_shot, doubled = traces.shape
    rays = ray_phase.shape[0]
    group = 4
    value = pltpu.VMEM((2, group * per_shot, 2 * rays), BF16)
    return pl.pallas_call(
        functools.partial(stack_kernel, group),
        out_shape=(
            jax.ShapeDtypeStruct((32, 2, 16, rays), F32),
            jax.ShapeDtypeStruct((32, 2, 16, rays), BF16),
        ),
        in_specs=[HBM] * 5,
        out_specs=(VMEM, VMEM),
        scratch_shapes=[
            pltpu.VMEM(traces.shape, BF16),
            pltpu.SMEM(window.shape, jnp.int32),
            pltpu.VMEM(slots.shape, jnp.int32),
            pltpu.VMEM(table.shape, BF16),
            pltpu.VMEM(ray_phase.shape, BF16),
            pltpu.VMEM((2 * rays, doubled), BF16),
            pltpu.VMEM((shots, 256, 2 * per_shot), BF16),
            value,
            value,
            pltpu.VMEM((16, 2 * P_SIZE, rays), F32),
            pltpu.SemaphoreType.DMA((4,)),
            pltpu.SemaphoreType.DMA((shots // group,)),
        ],
        compiler_params=pltpu.CompilerParams(vmem_limit_bytes=STACK_VMEM),
        name="stack",
    )(*[pltpu.with_memory_space_constraint(jnp.asarray(x), pltpu.HBM) for x in operands])


STACK_VMEM = 48 << 20
IMAGE_VMEM = 12 << 20


def spread_kernel(arrived_ref, out_ref):
    total = jnp.sum(arrived_ref[...].astype(F32), axis=0).astype(out_ref.dtype)
    for i in range(out_ref.shape[0]):
        out_ref[i] = total


def spread(arrived):
    return pl.pallas_call(
        spread_kernel,
        out_shape=jax.ShapeDtypeStruct((32,) + arrived.shape[1:], BF16),
        in_specs=[VMEM],
        out_specs=VMEM,
        compiler_params=pltpu.CompilerParams(vmem_limit_bytes=8 << 20),
        name="spread",
    )(arrived)


def select(index_ref, table_ref, lane_ref):
    rays = table_ref.shape[-1]
    depths = index_ref.shape[1]
    lane_ref[:WIN_OWN, :depths] = index_ref[...]
    spread_out = lane_ref[...]
    lane = lax.broadcasted_iota(jnp.int32, (1, 128), 1)
    index = jnp.zeros((1, 128), jnp.int32)
    for wl in range(WIN_OWN):
        moved = pltpu.roll(spread_out, wl * depths, 1)[wl : wl + 1]
        here = (lane >= wl * depths) & (lane < (wl + 1) * depths)
        index = jnp.where(here, moved, index)
    rows = lax.broadcasted_iota(jnp.int32, (rays, 128), 0)
    pick = jnp.transpose((rows == index).astype(F32)).astype(BF16)
    group = lax.broadcasted_iota(jnp.int32, (depths, 512), 1) // P_SIZE % WIN_OWN
    table = table_ref[...].reshape(512, rays)
    waves = lax.dot_general(pick, table, NT, preferred_element_type=F32)
    wave = waves[:depths]
    for wl in range(1, WIN_OWN):
        wave = jnp.where(group == wl, waves[wl * depths : (wl + 1) * depths], wave)
    return wave.astype(BF16)


def multiply(far, other, wave, basis_ref, out_ref):
    side, core = beam_position()
    chunk = (1 - side if far else side) * 2 + (1 - core if other else core)
    laterals = out_ref.shape[1]
    width = 512
    for i in range(laterals // width):
        columns = pl.ds(pl.multiple_of(chunk * laterals + i * width, width), width)
        basis = basis_ref[:, :, columns].reshape(512, width)
        out_ref[:, i * width : (i + 1) * width] = jnp.dot(
            wave, basis, preferred_element_type=F32
        )


def first_kernel(index_ref, table_ref, basis_ref, out_ref, wave_ref, lane_ref):
    wave_ref[...] = select(index_ref, table_ref, lane_ref)
    multiply(True, True, wave_ref[...], basis_ref, out_ref)


def later_kernel(far, other, wave_ref, basis_ref, out_ref):
    multiply(far, other, wave_ref[...], basis_ref, out_ref)


def image_call(kernel, depths, laterals, basis, wave_out, *operands):
    shape = jax.ShapeDtypeStruct((depths, laterals), F32)
    wave = jax.ShapeDtypeStruct((depths, 512), BF16)
    return pl.pallas_call(
        kernel,
        out_shape=(shape, wave) if wave_out else shape,
        in_specs=[VMEM] * (len(operands) + 1),
        out_specs=(VMEM, VMEM) if wave_out else VMEM,
        scratch_shapes=[pltpu.VMEM((8, 128), jnp.int32)] * wave_out,
        compiler_params=pltpu.CompilerParams(vmem_limit_bytes=IMAGE_VMEM),
        cost_estimate=pl.CostEstimate(
            flops=2 * depths * 512 * laterals, bytes_accessed=1024 * laterals, transcendentals=0
        ),
    )(*operands, basis)


def body(traces, shot_window, trace_slot, ray_phase, ray_index, beam_basis):
    shots, per_shot, _ = traces.shape
    rays = ray_phase.shape[0]
    depths = ray_index.shape[1]
    slabs, beams = lax.axis_size("slab"), lax.axis_size("beam")
    devices = slabs * beams
    chunk = beam_basis.shape[2] // beams
    scale = (shots * devices * per_shot / (WIN_OWN * beams)) ** -0.5
    partner = [(i, i ^ 1) for i in range(devices)]
    distant = [(i, i ^ 2) for i in range(devices)]
    same_core = [list(range(core, devices, 2)) for core in range(2)]

    mine, other = stack(shot_window, trace_slot, slant_table(scale), ray_phase, traces)
    other = lax.ppermute(other, AXES, partner)
    both = (mine + other.astype(F32)).astype(BF16).reshape(2 * slabs, 16, rays)
    arrived = lax.all_to_all(both, AXES, 0, 0, axis_index_groups=same_core, tiled=True)
    table = lax.all_to_all(spread(arrived), "slab", 0, 0, tiled=True)

    far_other, wave = image_call(first_kernel, depths, chunk, beam_basis, True, ray_index, table)
    call = lambda far, other, wave: image_call(
        functools.partial(later_kernel, far, other), depths, chunk, beam_basis, False, wave
    )
    far_other = lax.ppermute(far_other, AXES, partner)
    far_mine = call(True, False, wave)
    far = (far_mine + far_other).astype(BF16)
    far = lax.ppermute(far, AXES, distant)
    near_other = call(False, True, wave)
    near_other = lax.ppermute(near_other, AXES, partner)
    near_mine = call(False, False, wave)
    return near_mine + near_other + far.astype(F32)


def solution(mesh):
    in_specs = (
        P(("slab", "beam"), None, None),
        P(("slab", "beam")),
        P(("slab", "beam"), None),
        P(),
        P("beam", "slab"),
        P(None, "beam", None),
    )
    return jax.shard_map(
        body, mesh=mesh, in_specs=in_specs, out_specs=P("slab", "beam"), check_vma=False
    )
```

```python
import functools
import math

import jax
import jax.numpy as jnp
import numpy as np
from jax import lax
from jax.experimental import pallas as pl
from jax.experimental.pallas import tpu as pltpu
from jax.sharding import PartitionSpec as P


P_SIZE = 64
K = 64
WIN_OWN = 4
AXES = ("slab", "beam")
BF16 = jnp.bfloat16
F32 = jnp.float32
NT = (((1,), (1,)), ((), ()))
HBM = pl.BlockSpec(memory_space=pltpu.HBM)
VMEM = pl.BlockSpec(memory_space=pltpu.VMEM)


def slant_table(scale):
    steps = np.arange(P_SIZE)[:, None] * np.arange(K)[None, :] % K
    angles = steps * (2.0 * math.pi / K)
    full = (np.concatenate([np.cos(angles), np.sin(angles)]) * scale).astype(np.float32)
    high = full.astype(BF16)
    low = (full - high.astype(np.float32)).astype(BF16)
    return np.pad(np.concatenate([high, low]), ((0, 0), (0, 128 - K)))


def split(value):
    high = value.astype(BF16)
    return high, (value - high.astype(F32)).astype(BF16)


def beam_position():
    position = lax.axis_index("beam")
    return lax.div(position, 2), lax.rem(position, 2)


def order_shots(window_ref, order_ref, core):
    shots = order_ref.shape[0]
    others = jnp.int32(0)
    for shot in range(shots):
        away = ((window_ref[shot] >> 2) & 1) ^ core
        order_ref[jnp.where(away == 1, others, shots // 2 + shot - others)] = shot
        others = others + away


def accumulate(groups, base, window_ref, order_ref, buffer, weight_ref, factor_ref, high_ref, low_ref, acc_ref, wait):
    per_shot, doubled = buffer.shape[1:]
    rays = weight_ref.shape[0] // 2

    def slant(slot, rows):
        high = jnp.concatenate([high_ref[rows, :rays], high_ref[rows, rays:]], axis=0)
        low = jnp.concatenate([low_ref[rows, :rays], low_ref[rows, rays:]], axis=0)
        one = jnp.dot(factor_ref[slot], high, preferred_element_type=F32)
        two = jnp.dot(factor_ref[slot, :128], low, preferred_element_type=F32)
        window = window_ref[order_ref[base + slot]]
        acc_ref[(window >> 3) * WIN_OWN + (window & 3)] += one[:128] + one[128:] + two

    pending, first = [], 0
    for group in groups:
        wait(first, group)
        samples = buffer[base + first : base + first + group].reshape(group * per_shot, doubled)
        value = lax.dot_general(samples, weight_ref[...], NT, preferred_element_type=F32)
        all_rows = slice(first * per_shot, (first + group) * per_shot)
        high_ref[all_rows], low_ref[all_rows] = split(value)
        for slot in pending:
            slant(slot, slice(slot * per_shot, (slot + 1) * per_shot))
        pending = range(first, first + group)
        first += group
    for slot in pending:
        slant(slot, slice(slot * per_shot, (slot + 1) * per_shot))


def put_sums(acc_ref, out_ref):
    rays = out_ref.shape[-1]
    for side in range(2):
        for wl in range(WIN_OWN):
            for h in range(2):
                at = h * 16 + wl * 4
                block = acc_ref[side * 4 + wl, h * 64 : (h + 1) * 64]
                out_ref[at : at + 4, side] = block.astype(out_ref.dtype).reshape(4, 16, rays)


def other_kernel(
    window_hbm, slot_hbm, table_hbm, ray_hbm, trace_hbm, out_ref, buffer, weight_ref, mine_ref,
    window_ref, order_ref, slot_ref, table_ref, ray_ref, factor_ref, high_ref, low_ref, acc_ref,
    sems, trace_sems,
):
    rays, doubled = ray_ref.shape
    half = doubled // 2
    shots, per_shot, _ = trace_hbm.shape
    _, core = beam_position()
    pairs = ((window_hbm, window_ref), (slot_hbm, slot_ref), (table_hbm, table_ref), (ray_hbm, ray_ref))
    small = [pltpu.make_async_copy(a, b, sems.at[i]) for i, (a, b) in enumerate(pairs)]
    for copy in small:
        copy.start()
    acc_ref[...] = jnp.zeros_like(acc_ref)
    small[0].wait()
    order_shots(window_ref, order_ref, core)
    load = lambda shot, slot: pltpu.make_async_copy(
        trace_hbm.at[shot], buffer.at[slot], trace_sems.at[slot]
    )
    for slot in range(shots):
        load(order_ref[slot], slot).start()

    small[1].wait()
    small[2].wait()
    slot_rows = lax.broadcasted_iota(jnp.int32, (128, per_shot), 0)

    def build(target, base):
        for first in range(0, shots // 2, 2):
            picks = []
            for slot in (base + first, base + first + 1):
                slots = slot_ref[pl.ds(order_ref[slot], 1), :]
                picks.append((slot_rows == slots).astype(F32).astype(BF16))
            both = jnp.dot(
                table_ref[...], jnp.concatenate(picks, axis=1), preferred_element_type=F32
            ).astype(BF16)
            for i in range(2):
                left = both[:, i * per_shot : (i + 1) * per_shot]
                target[first + i, :, :per_shot] = left
                target[first + i, :, per_shot:] = jnp.concatenate(
                    [left[64:128], -left[:64], left[192:], -left[128:192]], axis=0
                )

    build(factor_ref, 0)
    build(mine_ref, shots // 2)
    small[3].wait()
    weight_ref[:rays, :half] = ray_ref[:, :half]
    weight_ref[:rays, half:] = -ray_ref[:, half:]
    weight_ref[rays:, :half] = ray_ref[:, half:]
    weight_ref[rays:, half:] = ray_ref[:, :half]

    def wait(first, count):
        for slot in range(first, first + count):
            load(0, slot).wait()

    accumulate(
        (4, 4), 0, window_ref, order_ref, buffer, weight_ref, factor_ref, high_ref, low_ref,
        acc_ref, wait,
    )
    put_sums(acc_ref, out_ref)
    wait(shots // 2, shots // 2)


def mine_kernel(
    window_hbm, buffer, weight_ref, factor_ref, out_ref, window_ref, order_ref, high_ref,
    low_ref, acc_ref, sem,
):
    copy = pltpu.make_async_copy(window_hbm, window_ref, sem)
    copy.start()
    acc_ref[...] = jnp.zeros_like(acc_ref)
    _, core = beam_position()
    copy.wait()
    order_shots(window_ref, order_ref, core)
    accumulate(
        (8,), 8, window_ref, order_ref, buffer, weight_ref, factor_ref, high_ref, low_ref,
        acc_ref, lambda first, count: None,
    )
    put_sums(acc_ref, out_ref)


def stack(*operands):
    operands = [pltpu.with_memory_space_constraint(jnp.asarray(x), pltpu.HBM) for x in operands]
    window, slots, table, ray_phase, traces = operands
    shots, per_shot, doubled = traces.shape
    rays = ray_phase.shape[0]
    value = pltpu.VMEM((shots // 2 * per_shot, 2 * rays), BF16)
    scalars = pltpu.SMEM(window.shape, jnp.int32)
    acc = pltpu.VMEM((8, 2 * P_SIZE, rays), F32)
    shape = jax.ShapeDtypeStruct
    factor = shape((shots // 2, 256, 2 * per_shot), BF16)
    other, buffer, weight, factor = pl.pallas_call(
        other_kernel,
        out_shape=(
            shape((32, 2, 16, rays), BF16),
            shape(traces.shape, BF16),
            shape((2 * rays, doubled), BF16),
            factor,
        ),
        in_specs=[HBM] * 5,
        out_specs=(VMEM,) * 4,
        scratch_shapes=[
            scalars,
            scalars,
            pltpu.VMEM(slots.shape, jnp.int32),
            pltpu.VMEM(table.shape, BF16),
            pltpu.VMEM(ray_phase.shape, BF16),
            pltpu.VMEM(factor.shape, BF16),
            value,
            value,
            acc,
            pltpu.SemaphoreType.DMA((4,)),
            pltpu.SemaphoreType.DMA((shots,)),
        ],
        compiler_params=pltpu.CompilerParams(vmem_limit_bytes=STACK_VMEM),
        name="stack_other",
    )(*operands)
    mine = lambda: pl.pallas_call(
        mine_kernel,
        out_shape=shape((32, 2, 16, rays), F32),
        in_specs=[HBM, VMEM, VMEM, VMEM],
        out_specs=VMEM,
        scratch_shapes=[scalars, scalars, value, value, acc, pltpu.SemaphoreType.DMA],
        compiler_params=pltpu.CompilerParams(vmem_limit_bytes=MINE_VMEM),
        cost_estimate=pl.CostEstimate(flops=2 << 30, bytes_accessed=8 << 20, transcendentals=0),
        name="stack_mine",
    )(window, buffer, weight, factor)
    return other, mine


STACK_VMEM = 32 << 20
MINE_VMEM = 24 << 20
IMAGE_VMEM = 12 << 20


def spread_kernel(arrived_ref, out_ref):
    total = jnp.sum(arrived_ref[...].astype(F32), axis=0).astype(out_ref.dtype)
    for i in range(out_ref.shape[0]):
        out_ref[i] = total


def spread(arrived):
    return pl.pallas_call(
        spread_kernel,
        out_shape=jax.ShapeDtypeStruct((32,) + arrived.shape[1:], BF16),
        in_specs=[VMEM],
        out_specs=VMEM,
        compiler_params=pltpu.CompilerParams(vmem_limit_bytes=8 << 20),
        name="spread",
    )(arrived)


def select(index_ref, table_ref, lane_ref):
    rays = table_ref.shape[-1]
    depths = index_ref.shape[1]
    lane_ref[:WIN_OWN, :depths] = index_ref[...]
    spread_out = lane_ref[...]
    lane = lax.broadcasted_iota(jnp.int32, (1, 128), 1)
    index = jnp.zeros((1, 128), jnp.int32)
    for wl in range(WIN_OWN):
        moved = pltpu.roll(spread_out, wl * depths, 1)[wl : wl + 1]
        here = (lane >= wl * depths) & (lane < (wl + 1) * depths)
        index = jnp.where(here, moved, index)
    rows = lax.broadcasted_iota(jnp.int32, (rays, 128), 0)
    pick = jnp.transpose((rows == index).astype(F32)).astype(BF16)
    group = lax.broadcasted_iota(jnp.int32, (depths, 512), 1) // P_SIZE % WIN_OWN
    table = table_ref[...].reshape(512, rays)
    waves = lax.dot_general(pick, table, NT, preferred_element_type=F32)
    wave = waves[:depths]
    for wl in range(1, WIN_OWN):
        wave = jnp.where(group == wl, waves[wl * depths : (wl + 1) * depths], wave)
    return wave.astype(BF16)


def multiply(far, other, wave, basis_ref, out_ref):
    side, core = beam_position()
    chunk = (1 - side if far else side) * 2 + (1 - core if other else core)
    laterals = out_ref.shape[1]
    width = 512
    for i in range(laterals // width):
        columns = pl.ds(pl.multiple_of(chunk * laterals + i * width, width), width)
        basis = basis_ref[:, :, columns].reshape(512, width)
        out_ref[:, i * width : (i + 1) * width] = jnp.dot(
            wave, basis, preferred_element_type=F32
        )


def first_kernel(index_ref, table_ref, basis_ref, out_ref, wave_ref, lane_ref):
    wave_ref[...] = select(index_ref, table_ref, lane_ref)
    multiply(True, True, wave_ref[...], basis_ref, out_ref)


def later_kernel(far, other, wave_ref, basis_ref, out_ref):
    multiply(far, other, wave_ref[...], basis_ref, out_ref)


def image_call(kernel, depths, laterals, basis, wave_out, *operands):
    shape = jax.ShapeDtypeStruct((depths, laterals), F32)
    wave = jax.ShapeDtypeStruct((depths, 512), BF16)
    return pl.pallas_call(
        kernel,
        out_shape=(shape, wave) if wave_out else shape,
        in_specs=[VMEM] * (len(operands) + 1),
        out_specs=(VMEM, VMEM) if wave_out else VMEM,
        scratch_shapes=[pltpu.VMEM((8, 128), jnp.int32)] * wave_out,
        compiler_params=pltpu.CompilerParams(vmem_limit_bytes=IMAGE_VMEM),
        cost_estimate=pl.CostEstimate(
            flops=2 * depths * 512 * laterals, bytes_accessed=1024 * laterals, transcendentals=0
        ),
    )(*operands, basis)


def body(traces, shot_window, trace_slot, ray_phase, ray_index, beam_basis):
    shots, per_shot, _ = traces.shape
    rays = ray_phase.shape[0]
    depths = ray_index.shape[1]
    slabs, beams = lax.axis_size("slab"), lax.axis_size("beam")
    devices = slabs * beams
    chunk = beam_basis.shape[2] // beams
    scale = (shots * devices * per_shot / (WIN_OWN * beams)) ** -0.5
    partner = [(i, i ^ 1) for i in range(devices)]
    distant = [(i, i ^ 2) for i in range(devices)]
    same_core = [list(range(core, devices, 2)) for core in range(2)]

    other, mine = stack(shot_window, trace_slot, slant_table(scale), ray_phase, traces)
    other = lax.ppermute(other, AXES, partner)
    both = (mine() + other.astype(F32)).astype(BF16).reshape(2 * slabs, 16, rays)
    arrived = lax.all_to_all(both, AXES, 0, 0, axis_index_groups=same_core, tiled=True)
    table = lax.all_to_all(spread(arrived), "slab", 0, 0, tiled=True)

    far_other, wave = image_call(first_kernel, depths, chunk, beam_basis, True, ray_index, table)
    call = lambda far, other, wave: image_call(
        functools.partial(later_kernel, far, other), depths, chunk, beam_basis, False, wave
    )
    far_other = lax.ppermute(far_other, AXES, partner)
    far_mine = call(True, False, wave)
    far = (far_mine + far_other).astype(BF16)
    far = lax.ppermute(far, AXES, distant)
    near_other = call(False, True, wave)
    near_other = lax.ppermute(near_other, AXES, partner)
    near_mine = call(False, False, wave)
    return near_mine + near_other + far.astype(F32)


def solution(mesh):
    in_specs = (
        P(("slab", "beam"), None, None),
        P(("slab", "beam")),
        P(("slab", "beam"), None),
        P(),
        P("beam", "slab"),
        P(None, "beam", None),
    )
    return jax.shard_map(
        body, mesh=mesh, in_specs=in_specs, out_specs=P("slab", "beam"), check_vma=False
    )
```

```python
import functools
import math

import jax
import jax.numpy as jnp
import numpy as np
from jax import lax
from jax.experimental import pallas as pl
from jax.experimental.pallas import tpu as pltpu
from jax.sharding import PartitionSpec as P


P_SIZE = 64
K = 64
WIN_OWN = 4
AXES = ("slab", "beam")
BF16 = jnp.bfloat16
F32 = jnp.float32
NT = (((1,), (1,)), ((), ()))
HBM = pl.BlockSpec(memory_space=pltpu.HBM)
VMEM = pl.BlockSpec(memory_space=pltpu.VMEM)


def slant_table(scale):
    steps = np.arange(P_SIZE)[:, None] * np.arange(K)[None, :] % K
    angles = steps * (2.0 * math.pi / K)
    full = (np.concatenate([np.cos(angles), np.sin(angles)]) * scale).astype(np.float32)
    high = full.astype(BF16)
    low = (full - high.astype(np.float32)).astype(BF16)
    return np.pad(np.concatenate([high, low]), ((0, 0), (0, 128 - K)))


def split(value):
    high = value.astype(BF16)
    return high, (value - high.astype(F32)).astype(BF16)


def beam_position():
    position = lax.axis_index("beam")
    return lax.div(position, 2), lax.rem(position, 2)


def order_shots(window_ref, order_ref, core):
    shots = order_ref.shape[0]
    others = jnp.int32(0)
    for shot in range(shots):
        away = ((window_ref[shot] >> 2) & 1) ^ core
        order_ref[jnp.where(away == 1, others, shots // 2 + shot - others)] = shot
        others = others + away


def accumulate(groups, base, window_ref, order_ref, buffer, weight_ref, factor_ref, high_ref, low_ref, acc_ref, wait, ready=None):
    per_shot, doubled = buffer.shape[1:]
    rays = weight_ref.shape[0] // 2

    def slant(slot, rows):
        high = jnp.concatenate([high_ref[rows, :rays], high_ref[rows, rays:]], axis=0)
        low = jnp.concatenate([low_ref[rows, :rays], low_ref[rows, rays:]], axis=0)
        one = jnp.dot(factor_ref[slot], high, preferred_element_type=F32)
        two = jnp.dot(factor_ref[slot, :128], low, preferred_element_type=F32)
        window = window_ref[order_ref[base + slot]]
        acc_ref[(window >> 3) * WIN_OWN + (window & 3)] += one[:128] + one[128:] + two

    pending, first = [], 0
    for group in groups:
        wait(first, group)
        samples = buffer[base + first : base + first + group].reshape(group * per_shot, doubled)
        value = lax.dot_general(samples, weight_ref[...], NT, preferred_element_type=F32)
        all_rows = slice(first * per_shot, (first + group) * per_shot)
        high_ref[all_rows], low_ref[all_rows] = split(value)
        if first == 0 and ready is not None:
            ready()
        for slot in pending:
            slant(slot, slice(slot * per_shot, (slot + 1) * per_shot))
        pending = range(first, first + group)
        first += group
    for slot in pending:
        slant(slot, slice(slot * per_shot, (slot + 1) * per_shot))


def put_sums(acc_ref, out_ref):
    for side in range(2):
        for wl in range(WIN_OWN):
            for h in range(2):
                for quarter in range(4):
                    at = h * 64 + quarter * 16
                    block = acc_ref[side * 4 + wl, at : at + 16]
                    slab = h * 16 + wl * 4 + quarter
                    out_ref[slab ^ FIRST_SUM[0], side ^ FIRST_SUM[1]] = block.astype(out_ref.dtype)


def other_kernel(
    window_hbm, slot_hbm, table_hbm, ray_hbm, trace_hbm, out_ref, buffer, weight_ref, mine_ref,
    window_ref, order_ref, slot_ref, table_ref, ray_ref, factor_ref, high_ref, low_ref, acc_ref,
    sems, trace_sems,
):
    rays, doubled = ray_ref.shape
    half = doubled // 2
    shots, per_shot, _ = trace_hbm.shape
    _, core = beam_position()
    pairs = ((window_hbm, window_ref), (slot_hbm, slot_ref), (table_hbm, table_ref), (ray_hbm, ray_ref))
    small = [pltpu.make_async_copy(a, b, sems.at[i]) for i, (a, b) in enumerate(pairs)]
    for copy in small:
        copy.start()
    acc_ref[...] = jnp.zeros_like(acc_ref)
    small[0].wait()
    order_shots(window_ref, order_ref, core)
    load = lambda shot, slot: pltpu.make_async_copy(
        trace_hbm.at[shot], buffer.at[slot], trace_sems.at[slot]
    )
    for slot in range(shots):
        load(order_ref[slot], slot).start(priority=1)

    small[1].wait()
    small[2].wait()
    slot_rows = lax.broadcasted_iota(jnp.int32, (128, per_shot), 0)

    def build(target, base):
        for first in range(0, shots // 2, 2):
            picks = []
            for slot in (base + first, base + first + 1):
                slots = slot_ref[pl.ds(order_ref[slot], 1), :]
                picks.append((slot_rows == slots).astype(F32).astype(BF16))
            both = jnp.dot(
                table_ref[...], jnp.concatenate(picks, axis=1), preferred_element_type=F32
            ).astype(BF16)
            for i in range(2):
                left = both[:, i * per_shot : (i + 1) * per_shot]
                target[first + i, :, :per_shot] = left
                target[first + i, :, per_shot:] = jnp.concatenate(
                    [left[64:128], -left[:64], left[192:], -left[128:192]], axis=0
                )

    build(factor_ref, 0)
    build(mine_ref, shots // 2)
    small[3].wait()
    weight_ref[:rays, :half] = ray_ref[:, :half]
    weight_ref[:rays, half:] = -ray_ref[:, half:]
    weight_ref[rays:, :half] = ray_ref[:, half:]
    weight_ref[rays:, half:] = ray_ref[:, :half]

    def wait(first, count):
        for slot in range(first, first + count):
            load(0, slot).wait()

    accumulate(
        (4, 4), 0, window_ref, order_ref, buffer, weight_ref, factor_ref, high_ref, low_ref,
        acc_ref, wait,
    )
    put_sums(acc_ref, out_ref)
    wait(shots // 2, shots // 2)


def mine_kernel(
    window_hbm, buffer, weight_ref, factor_ref, out_ref, window_ref, order_ref, high_ref,
    low_ref, acc_ref, sem,
):
    copy = pltpu.make_async_copy(window_hbm, window_ref, sem)
    copy.start()
    acc_ref[...] = jnp.zeros_like(acc_ref)
    _, core = beam_position()

    def ready():
        copy.wait()
        order_shots(window_ref, order_ref, core)

    accumulate(
        (4, 4), 8, window_ref, order_ref, buffer, weight_ref, factor_ref, high_ref, low_ref,
        acc_ref, lambda first, count: None, ready,
    )
    put_sums(acc_ref, out_ref)


def stack(*operands):
    operands = [pltpu.with_memory_space_constraint(jnp.asarray(x), pltpu.HBM) for x in operands]
    window, slots, table, ray_phase, traces = operands
    shots, per_shot, doubled = traces.shape
    rays = ray_phase.shape[0]
    value = pltpu.VMEM((shots // 2 * per_shot, 2 * rays), BF16)
    scalars = pltpu.SMEM(window.shape, jnp.int32)
    acc = pltpu.VMEM((8, 2 * P_SIZE, rays), F32)
    shape = jax.ShapeDtypeStruct
    factor = shape((shots // 2, 256, 2 * per_shot), BF16)
    other, buffer, weight, factor = pl.pallas_call(
        other_kernel,
        out_shape=(
            shape((32, 2, 16, rays), BF16),
            shape(traces.shape, BF16),
            shape((2 * rays, doubled), BF16),
            factor,
        ),
        in_specs=[HBM] * 5,
        out_specs=(VMEM,) * 4,
        scratch_shapes=[
            scalars,
            scalars,
            pltpu.VMEM(slots.shape, jnp.int32),
            pltpu.VMEM(table.shape, BF16),
            pltpu.VMEM(ray_phase.shape, BF16),
            pltpu.VMEM(factor.shape, BF16),
            value,
            value,
            acc,
            pltpu.SemaphoreType.DMA((4,)),
            pltpu.SemaphoreType.DMA((shots,)),
        ],
        compiler_params=pltpu.CompilerParams(vmem_limit_bytes=STACK_VMEM),
        name="stack_other",
    )(*operands)
    mine = lambda: pl.pallas_call(
        mine_kernel,
        out_shape=shape((32, 2, 16, rays), F32),
        in_specs=[HBM, VMEM, VMEM, VMEM],
        out_specs=VMEM,
        scratch_shapes=[scalars, scalars, value, value, acc, pltpu.SemaphoreType.DMA],
        compiler_params=pltpu.CompilerParams(vmem_limit_bytes=MINE_VMEM),
        cost_estimate=pl.CostEstimate(flops=2 << 30, bytes_accessed=8 << 20, transcendentals=0),
        name="stack_mine",
    )(window, buffer, weight, factor)
    return other, mine


FIRST_SUM = (20, 1)
FIRST_SPREAD = 20
STACK_VMEM = 32 << 20
MINE_VMEM = 24 << 20
IMAGE_VMEM = 12 << 20


def spread_kernel(arrived_ref, out_ref):
    total = jnp.sum(arrived_ref[...].astype(F32), axis=0).astype(out_ref.dtype)
    for i in range(out_ref.shape[0]):
        out_ref[i] = total


def spread(arrived):
    return pl.pallas_call(
        spread_kernel,
        out_shape=jax.ShapeDtypeStruct((32,) + arrived.shape[1:], BF16),
        in_specs=[VMEM],
        out_specs=VMEM,
        compiler_params=pltpu.CompilerParams(vmem_limit_bytes=8 << 20),
        name="spread",
    )(arrived)


def select(index_ref, table_ref, lane_ref):
    rays = table_ref.shape[-1]
    depths = index_ref.shape[1]
    lane_ref[:WIN_OWN, :depths] = index_ref[...]
    spread_out = lane_ref[...]
    lane = lax.broadcasted_iota(jnp.int32, (1, 128), 1)
    index = jnp.zeros((1, 128), jnp.int32)
    for wl in range(WIN_OWN):
        moved = pltpu.roll(spread_out, wl * depths, 1)[wl : wl + 1]
        here = (lane >= wl * depths) & (lane < (wl + 1) * depths)
        index = jnp.where(here, moved, index)
    rows = lax.broadcasted_iota(jnp.int32, (rays, 128), 0)
    pick = jnp.transpose((rows == index).astype(F32)).astype(BF16)
    group = lax.broadcasted_iota(jnp.int32, (depths, 512), 1) // P_SIZE % WIN_OWN
    table = jnp.concatenate([table_ref[i ^ FIRST_SPREAD] for i in range(32)], axis=0)
    waves = lax.dot_general(pick, table, NT, preferred_element_type=F32)
    wave = waves[:depths]
    for wl in range(1, WIN_OWN):
        wave = jnp.where(group == wl, waves[wl * depths : (wl + 1) * depths], wave)
    return wave.astype(BF16)


def multiply(far, other, wave, basis_ref, out_ref):
    side, core = beam_position()
    chunk = (1 - side if far else side) * 2 + (1 - core if other else core)
    laterals = out_ref.shape[1]
    width = 512
    for i in range(laterals // width):
        columns = pl.ds(pl.multiple_of(chunk * laterals + i * width, width), width)
        basis = basis_ref[:, :, columns].reshape(512, width)
        out_ref[:, i * width : (i + 1) * width] = jnp.dot(
            wave, basis, preferred_element_type=F32
        )


def first_kernel(index_ref, table_ref, basis_ref, out_ref, wave_ref, lane_ref):
    wave_ref[...] = select(index_ref, table_ref, lane_ref)
    multiply(True, True, wave_ref[...], basis_ref, out_ref)


def later_kernel(far, other, wave_ref, basis_ref, out_ref):
    multiply(far, other, wave_ref[...], basis_ref, out_ref)


def image_call(kernel, depths, laterals, basis, wave_out, *operands):
    shape = jax.ShapeDtypeStruct((depths, laterals), F32)
    wave = jax.ShapeDtypeStruct((depths, 512), BF16)
    return pl.pallas_call(
        kernel,
        out_shape=(shape, wave) if wave_out else shape,
        in_specs=[VMEM] * (len(operands) + 1),
        out_specs=(VMEM, VMEM) if wave_out else VMEM,
        scratch_shapes=[pltpu.VMEM((8, 128), jnp.int32)] * wave_out,
        compiler_params=pltpu.CompilerParams(vmem_limit_bytes=IMAGE_VMEM),
        cost_estimate=pl.CostEstimate(
            flops=2 * depths * 512 * laterals, bytes_accessed=1024 * laterals, transcendentals=0
        ),
    )(*operands, basis)


def body(traces, shot_window, trace_slot, ray_phase, ray_index, beam_basis):
    shots, per_shot, _ = traces.shape
    rays = ray_phase.shape[0]
    depths = ray_index.shape[1]
    slabs, beams = lax.axis_size("slab"), lax.axis_size("beam")
    devices = slabs * beams
    chunk = beam_basis.shape[2] // beams
    scale = (shots * devices * per_shot / (WIN_OWN * beams)) ** -0.5
    partner = [(i, i ^ 1) for i in range(devices)]
    distant = [(i, i ^ 2) for i in range(devices)]
    first = FIRST_SUM[0] * 2 + FIRST_SUM[1]
    same_core = [[(i ^ first) * 2 + core for i in range(devices // 2)] for core in range(2)]
    same_beam = [[(i ^ FIRST_SPREAD) * beams + beam for i in range(slabs)] for beam in range(beams)]

    other, mine = stack(shot_window, trace_slot, slant_table(scale), ray_phase, traces)
    other = lax.ppermute(other, AXES, partner)
    both = (mine() + other.astype(F32)).astype(BF16).reshape(2 * slabs, 16, rays)
    arrived = lax.all_to_all(both, AXES, 0, 0, axis_index_groups=same_core, tiled=True)
    table = lax.all_to_all(
        spread(arrived), AXES, 0, 0, axis_index_groups=same_beam, tiled=True
    )

    far_other, wave = image_call(first_kernel, depths, chunk, beam_basis, True, ray_index, table)
    call = lambda far, other, wave: image_call(
        functools.partial(later_kernel, far, other), depths, chunk, beam_basis, False, wave
    )
    far_other = lax.ppermute(far_other, AXES, partner)
    far_mine = call(True, False, wave)
    far = (far_mine + far_other).astype(BF16)
    far = lax.ppermute(far, AXES, distant)
    near_other = call(False, True, wave)
    near_other = lax.ppermute(near_other, AXES, partner)
    near_mine = call(False, False, wave)
    return near_mine + near_other + far.astype(F32)


def solution(mesh):
    in_specs = (
        P(("slab", "beam"), None, None),
        P(("slab", "beam")),
        P(("slab", "beam"), None),
        P(),
        P("beam", "slab"),
        P(None, "beam", None),
    )
    return jax.shard_map(
        body, mesh=mesh, in_specs=in_specs, out_specs=P("slab", "beam"), check_vma=False
    )
```

```python
import functools
import math

import jax
import jax.numpy as jnp
import numpy as np
from jax import lax
from jax.experimental import pallas as pl
from jax.experimental.pallas import tpu as pltpu
from jax.sharding import PartitionSpec as P


P_SIZE = 64
K = 64
WIN_OWN = 4
AXES = ("slab", "beam")
BF16 = jnp.bfloat16
F32 = jnp.float32
NT = (((1,), (1,)), ((), ()))
HBM = pl.BlockSpec(memory_space=pltpu.HBM)
VMEM = pl.BlockSpec(memory_space=pltpu.VMEM)


def slant_table(scale):
    steps = np.arange(P_SIZE)[:, None] * np.arange(K)[None, :] % K
    angles = steps * (2.0 * math.pi / K)
    full = (np.concatenate([np.cos(angles), np.sin(angles)]) * scale).astype(np.float32)
    high = full.astype(BF16)
    low = (full - high.astype(np.float32)).astype(BF16)
    return np.pad(np.concatenate([high, low]), ((0, 0), (0, 128 - K)))


def split(value):
    high = value.astype(BF16)
    return high, (value - high.astype(F32)).astype(BF16)


def beam_position():
    position = lax.axis_index("beam")
    return lax.div(position, 2), lax.rem(position, 2)


def order_shots(window_ref, order_ref, core):
    shots = order_ref.shape[0]
    others = jnp.int32(0)
    for shot in range(shots):
        away = ((window_ref[shot] >> 2) & 1) ^ core
        order_ref[jnp.where(away == 1, others, shots // 2 + shot - others)] = shot
        others = others + away


def accumulate(groups, base, window_ref, order_ref, buffer, weight_ref, factor_ref, high_ref, low_ref, acc_ref, wait, ready=None):
    per_shot, _ = buffer.shape[1:]
    rays = weight_ref.shape[0] // 2

    def slant(slot, rows):
        high = jnp.concatenate([high_ref[rows, :rays], high_ref[rows, rays:]], axis=0)
        low = jnp.concatenate([low_ref[rows, :rays], low_ref[rows, rays:]], axis=0)
        one = jnp.dot(factor_ref[slot], high, preferred_element_type=F32)
        two = jnp.dot(factor_ref[slot, :128], low, preferred_element_type=F32)
        window = window_ref[order_ref[base + slot]]
        acc_ref[(window >> 3) * WIN_OWN + (window & 3)] += one[:128] + one[128:] + two

    pending, first = [], 0
    for group in groups:
        wait(first, group)
        samples = jnp.concatenate(
            [buffer[order_ref[base + first + i]] for i in range(group)], axis=0
        )
        value = lax.dot_general(samples, weight_ref[...], NT, preferred_element_type=F32)
        all_rows = slice(first * per_shot, (first + group) * per_shot)
        high_ref[all_rows], low_ref[all_rows] = split(value)
        if first == 0 and ready is not None:
            ready()
        for slot in pending:
            slant(slot, slice(slot * per_shot, (slot + 1) * per_shot))
        pending = range(first, first + group)
        first += group
    for slot in pending:
        slant(slot, slice(slot * per_shot, (slot + 1) * per_shot))


def put_sums(acc_ref, out_ref):
    for side in range(2):
        for wl in range(WIN_OWN):
            for h in range(2):
                for quarter in range(4):
                    at = h * 64 + quarter * 16
                    block = acc_ref[side * 4 + wl, at : at + 16]
                    slab = h * 16 + wl * 4 + quarter
                    out_ref[slab ^ FIRST_SUM[0], side ^ FIRST_SUM[1]] = block.astype(out_ref.dtype)


def other_kernel(
    window_hbm, slot_hbm, table_hbm, ray_hbm, trace_hbm, out_ref, buffer, weight_ref, mine_ref,
    window_ref, order_ref, slot_ref, table_ref, ray_ref, factor_ref, high_ref, low_ref, acc_ref,
    sems, trace_sems,
):
    rays, doubled = ray_ref.shape
    half = doubled // 2
    shots, per_shot, _ = trace_hbm.shape
    _, core = beam_position()
    pairs = ((window_hbm, window_ref), (slot_hbm, slot_ref), (table_hbm, table_ref), (ray_hbm, ray_ref))
    small = [pltpu.make_async_copy(a, b, sems.at[i]) for i, (a, b) in enumerate(pairs)]
    for copy in small:
        copy.start()
    load = lambda shot: pltpu.make_async_copy(
        trace_hbm.at[shot], buffer.at[shot], trace_sems.at[shot]
    )
    for shot in range(shots):
        load(shot).start(priority=1)
    acc_ref[...] = jnp.zeros_like(acc_ref)
    small[0].wait()
    order_shots(window_ref, order_ref, core)

    small[1].wait()
    small[2].wait()
    slot_rows = lax.broadcasted_iota(jnp.int32, (128, per_shot), 0)

    def build(target, base):
        for first in range(0, shots // 2, 2):
            picks = []
            for slot in (base + first, base + first + 1):
                slots = slot_ref[pl.ds(order_ref[slot], 1), :]
                picks.append((slot_rows == slots).astype(F32).astype(BF16))
            both = jnp.dot(
                table_ref[...], jnp.concatenate(picks, axis=1), preferred_element_type=F32
            ).astype(BF16)
            for i in range(2):
                left = both[:, i * per_shot : (i + 1) * per_shot]
                target[first + i, :, :per_shot] = left
                target[first + i, :, per_shot:] = jnp.concatenate(
                    [left[64:128], -left[:64], left[192:], -left[128:192]], axis=0
                )

    build(factor_ref, 0)
    build(mine_ref, shots // 2)
    small[3].wait()
    weight_ref[:rays, :half] = ray_ref[:, :half]
    weight_ref[:rays, half:] = -ray_ref[:, half:]
    weight_ref[rays:, :half] = ray_ref[:, half:]
    weight_ref[rays:, half:] = ray_ref[:, :half]

    def wait(first, count):
        for slot in range(first, first + count):
            load(order_ref[slot]).wait()

    accumulate(
        (4, 4), 0, window_ref, order_ref, buffer, weight_ref, factor_ref, high_ref, low_ref,
        acc_ref, wait,
    )
    put_sums(acc_ref, out_ref)
    wait(shots // 2, shots // 2)


def mine_kernel(
    window_hbm, buffer, weight_ref, factor_ref, out_ref, window_ref, order_ref, high_ref,
    low_ref, acc_ref, sem,
):
    copy = pltpu.make_async_copy(window_hbm, window_ref, sem)
    copy.start()
    acc_ref[...] = jnp.zeros_like(acc_ref)
    _, core = beam_position()

    copy.wait()
    order_shots(window_ref, order_ref, core)
    accumulate(
        (4, 4), 8, window_ref, order_ref, buffer, weight_ref, factor_ref, high_ref, low_ref,
        acc_ref, lambda first, count: None,
    )
    put_sums(acc_ref, out_ref)


def stack(*operands):
    operands = [pltpu.with_memory_space_constraint(jnp.asarray(x), pltpu.HBM) for x in operands]
    window, slots, table, ray_phase, traces = operands
    shots, per_shot, doubled = traces.shape
    rays = ray_phase.shape[0]
    value = pltpu.VMEM((shots // 2 * per_shot, 2 * rays), BF16)
    scalars = pltpu.SMEM(window.shape, jnp.int32)
    acc = pltpu.VMEM((8, 2 * P_SIZE, rays), F32)
    shape = jax.ShapeDtypeStruct
    factor = shape((shots // 2, 256, 2 * per_shot), BF16)
    other, buffer, weight, factor = pl.pallas_call(
        other_kernel,
        out_shape=(
            shape((32, 2, 16, rays), BF16),
            shape(traces.shape, BF16),
            shape((2 * rays, doubled), BF16),
            factor,
        ),
        in_specs=[HBM] * 5,
        out_specs=(VMEM,) * 4,
        scratch_shapes=[
            scalars,
            scalars,
            pltpu.VMEM(slots.shape, jnp.int32),
            pltpu.VMEM(table.shape, BF16),
            pltpu.VMEM(ray_phase.shape, BF16),
            pltpu.VMEM(factor.shape, BF16),
            value,
            value,
            acc,
            pltpu.SemaphoreType.DMA((4,)),
            pltpu.SemaphoreType.DMA((shots,)),
        ],
        compiler_params=pltpu.CompilerParams(vmem_limit_bytes=STACK_VMEM),
        name="stack_other",
    )(*operands)
    mine = lambda: pl.pallas_call(
        mine_kernel,
        out_shape=shape((32, 2, 16, rays), F32),
        in_specs=[HBM, VMEM, VMEM, VMEM],
        out_specs=VMEM,
        scratch_shapes=[scalars, scalars, value, value, acc, pltpu.SemaphoreType.DMA],
        compiler_params=pltpu.CompilerParams(vmem_limit_bytes=MINE_VMEM),
        cost_estimate=pl.CostEstimate(flops=2 << 30, bytes_accessed=8 << 20, transcendentals=0),
        name="stack_mine",
    )(window, buffer, weight, factor)
    return other, mine


FIRST_SUM = (20, 1)
FIRST_SPREAD = 21
STACK_VMEM = 32 << 20
MINE_VMEM = 24 << 20
IMAGE_VMEM = 12 << 20


def spread_kernel(arrived_ref, out_ref):
    total = jnp.sum(arrived_ref[...].astype(F32), axis=0).astype(out_ref.dtype)
    for i in range(out_ref.shape[0]):
        out_ref[i] = total


def spread(arrived):
    return pl.pallas_call(
        spread_kernel,
        out_shape=jax.ShapeDtypeStruct((32,) + arrived.shape[1:], BF16),
        in_specs=[VMEM],
        out_specs=VMEM,
        compiler_params=pltpu.CompilerParams(vmem_limit_bytes=8 << 20),
        name="spread",
    )(arrived)


def select(index_ref, table_ref, lane_ref):
    rays = table_ref.shape[-1]
    depths = index_ref.shape[1]
    lane_ref[:WIN_OWN, :depths] = index_ref[...]
    spread_out = lane_ref[...]
    lane = lax.broadcasted_iota(jnp.int32, (1, 128), 1)
    index = jnp.zeros((1, 128), jnp.int32)
    for wl in range(WIN_OWN):
        moved = pltpu.roll(spread_out, wl * depths, 1)[wl : wl + 1]
        here = (lane >= wl * depths) & (lane < (wl + 1) * depths)
        index = jnp.where(here, moved, index)
    rows = lax.broadcasted_iota(jnp.int32, (rays, 128), 0)
    pick = jnp.transpose((rows == index).astype(F32)).astype(BF16)
    group = lax.broadcasted_iota(jnp.int32, (depths, 512), 1) // P_SIZE % WIN_OWN
    table = jnp.concatenate([table_ref[i ^ FIRST_SPREAD] for i in range(32)], axis=0)
    waves = lax.dot_general(pick, table, NT, preferred_element_type=F32)
    wave = waves[:depths]
    for wl in range(1, WIN_OWN):
        wave = jnp.where(group == wl, waves[wl * depths : (wl + 1) * depths], wave)
    return wave.astype(BF16)


def multiply(far, other, wave, basis_ref, out_ref):
    side, core = beam_position()
    chunk = (1 - side if far else side) * 2 + (1 - core if other else core)
    laterals = out_ref.shape[1]
    width = 512
    for i in range(laterals // width):
        columns = pl.ds(pl.multiple_of(chunk * laterals + i * width, width), width)
        basis = basis_ref[:, :, columns].reshape(512, width)
        out_ref[:, i * width : (i + 1) * width] = jnp.dot(
            wave, basis, preferred_element_type=F32
        )


def first_kernel(index_ref, table_ref, basis_ref, out_ref, wave_ref, lane_ref):
    wave_ref[...] = select(index_ref, table_ref, lane_ref)
    multiply(True, True, wave_ref[...], basis_ref, out_ref)


def later_kernel(far, other, wave_ref, basis_ref, out_ref):
    multiply(far, other, wave_ref[...], basis_ref, out_ref)


def image_call(kernel, depths, laterals, basis, wave_out, *operands):
    shape = jax.ShapeDtypeStruct((depths, laterals), F32)
    wave = jax.ShapeDtypeStruct((depths, 512), BF16)
    return pl.pallas_call(
        kernel,
        out_shape=(shape, wave) if wave_out else shape,
        in_specs=[VMEM] * (len(operands) + 1),
        out_specs=(VMEM, VMEM) if wave_out else VMEM,
        scratch_shapes=[pltpu.VMEM((8, 128), jnp.int32)] * wave_out,
        compiler_params=pltpu.CompilerParams(vmem_limit_bytes=IMAGE_VMEM),
        cost_estimate=pl.CostEstimate(
            flops=2 * depths * 512 * laterals, bytes_accessed=1024 * laterals, transcendentals=0
        ),
    )(*operands, basis)


def body(traces, shot_window, trace_slot, ray_phase, ray_index, beam_basis):
    shots, per_shot, _ = traces.shape
    rays = ray_phase.shape[0]
    depths = ray_index.shape[1]
    slabs, beams = lax.axis_size("slab"), lax.axis_size("beam")
    devices = slabs * beams
    chunk = beam_basis.shape[2] // beams
    scale = (shots * devices * per_shot / (WIN_OWN * beams)) ** -0.5
    partner = [(i, i ^ 1) for i in range(devices)]
    distant = [(i, i ^ 2) for i in range(devices)]
    first = FIRST_SUM[0] * 2 + FIRST_SUM[1]
    same_core = [[(i ^ first) * 2 + core for i in range(devices // 2)] for core in range(2)]
    same_beam = [[(i ^ FIRST_SPREAD) * beams + beam for i in range(slabs)] for beam in range(beams)]

    other, mine = stack(shot_window, trace_slot, slant_table(scale), ray_phase, traces)
    other = lax.ppermute(other, AXES, partner)
    both = (mine() + other.astype(F32)).astype(BF16).reshape(2 * slabs, 16, rays)
    arrived = lax.all_to_all(both, AXES, 0, 0, axis_index_groups=same_core, tiled=True)
    table = lax.all_to_all(
        spread(arrived), AXES, 0, 0, axis_index_groups=same_beam, tiled=True
    )

    far_other, wave = image_call(first_kernel, depths, chunk, beam_basis, True, ray_index, table)
    call = lambda far, other, wave: image_call(
        functools.partial(later_kernel, far, other), depths, chunk, beam_basis, False, wave
    )
    far_other = lax.ppermute(far_other, AXES, partner)
    far_mine = call(True, False, wave)
    far = (far_mine + far_other).astype(BF16)
    far = lax.ppermute(far, AXES, distant)
    near_other = call(False, True, wave)
    near_other = lax.ppermute(near_other, AXES, partner)
    near_mine = call(False, False, wave)
    return near_mine + near_other + far.astype(F32)


def solution(mesh):
    in_specs = (
        P(("slab", "beam"), None, None),
        P(("slab", "beam")),
        P(("slab", "beam"), None),
        P(),
        P("beam", "slab"),
        P(None, "beam", None),
    )
    return jax.shard_map(
        body, mesh=mesh, in_specs=in_specs, out_specs=P("slab", "beam"), check_vma=False
    )
```

```python
import functools
import math

import jax
import jax.numpy as jnp
import numpy as np
from jax import lax
from jax.experimental import pallas as pl
from jax.experimental.pallas import tpu as pltpu
from jax.sharding import PartitionSpec as P


P_SIZE = 64
K = 64
WIN_OWN = 4
AXES = ("slab", "beam")
BF16 = jnp.bfloat16
F32 = jnp.float32
NT = (((1,), (1,)), ((), ()))
HBM = pl.BlockSpec(memory_space=pltpu.HBM)
VMEM = pl.BlockSpec(memory_space=pltpu.VMEM)


def slant_table(scale):
    steps = np.arange(P_SIZE)[:, None] * np.arange(K)[None, :] % K
    angles = steps * (2.0 * math.pi / K)
    full = (np.concatenate([np.cos(angles), np.sin(angles)]) * scale).astype(np.float32)
    high = full.astype(BF16)
    low = (full - high.astype(np.float32)).astype(BF16)
    return np.pad(np.concatenate([high, low]), ((0, 0), (0, 128 - K)))


def split(value):
    high = value.astype(BF16)
    return high, (value - high.astype(F32)).astype(BF16)


def beam_position():
    position = lax.axis_index("beam")
    return lax.div(position, 2), lax.rem(position, 2)


def order_shots(window_ref, order_ref, core):
    shots = order_ref.shape[0]
    others = jnp.int32(0)
    for shot in range(shots):
        away = ((window_ref[shot] >> 2) & 1) ^ core
        order_ref[jnp.where(away == 1, others, shots // 2 + shot - others)] = shot
        others = others + away


def accumulate(
    groups, base, window_ref, order_ref, pick, weight_ref, factor_ref, high_ref, low_ref, acc_ref,
    wait, ready=None,
):
    per_shot = factor_ref.shape[2] // 2
    rays = weight_ref.shape[0] // 2

    def slant(slot, rows):
        high = jnp.concatenate([high_ref[rows, :rays], high_ref[rows, rays:]], axis=0)
        low = jnp.concatenate([low_ref[rows, :rays], low_ref[rows, rays:]], axis=0)
        one = jnp.dot(factor_ref[slot], high, preferred_element_type=F32)
        two = jnp.dot(factor_ref[slot, :128], low, preferred_element_type=F32)
        window = window_ref[order_ref[base + slot]]
        acc_ref[(window >> 3) * WIN_OWN + (window & 3)] += one[:128] + one[128:] + two

    pending, first = [], 0
    for group in groups:
        wait(first, group)
        samples = jnp.concatenate([pick(first + i) for i in range(group)], axis=0)
        value = lax.dot_general(samples, weight_ref[...], NT, preferred_element_type=F32)
        all_rows = slice(first * per_shot, (first + group) * per_shot)
        high_ref[all_rows], low_ref[all_rows] = split(value)
        if first == 0 and ready is not None:
            ready()
        for slot in pending:
            slant(slot, slice(slot * per_shot, (slot + 1) * per_shot))
        pending = range(first, first + group)
        first += group
    for slot in pending:
        slant(slot, slice(slot * per_shot, (slot + 1) * per_shot))


def put_sums(acc_ref, out_ref):
    for side in range(2):
        for wl in range(WIN_OWN):
            for h in range(2):
                for quarter in range(4):
                    at = h * 64 + quarter * 16
                    block = acc_ref[side * 4 + wl, at : at + 16]
                    slab = h * 16 + wl * 4 + quarter
                    out_ref[slab ^ FIRST_SUM[0], side ^ FIRST_SUM[1]] = block.astype(out_ref.dtype)


def other_kernel(
    window_hbm, slot_hbm, table_hbm, ray_hbm, trace_hbm, out_ref, kept_ref, weight_ref, mine_ref,
    buffer, window_ref, order_ref, slot_ref, table_ref, ray_ref, factor_ref, high_ref, low_ref,
    acc_ref, sems, trace_sems, kept_sems,
):
    rays, doubled = ray_ref.shape
    half = doubled // 2
    shots, per_shot, _ = trace_hbm.shape
    _, core = beam_position()
    pairs = ((window_hbm, window_ref), (slot_hbm, slot_ref), (table_hbm, table_ref), (ray_hbm, ray_ref))
    small = [pltpu.make_async_copy(a, b, sems.at[i]) for i, (a, b) in enumerate(pairs)]
    for copy in small:
        copy.start()
    load = lambda shot: pltpu.make_async_copy(
        trace_hbm.at[shot], buffer.at[shot], trace_sems.at[shot]
    )
    for shot in range(shots):
        load(shot).start(priority=1)
    acc_ref[...] = jnp.zeros_like(acc_ref)
    small[0].wait()
    order_shots(window_ref, order_ref, core)

    small[1].wait()
    small[2].wait()
    slot_rows = lax.broadcasted_iota(jnp.int32, (128, per_shot), 0)

    def build(target, base):
        for first in range(0, shots // 2, 2):
            picks = []
            for slot in (base + first, base + first + 1):
                slots = slot_ref[pl.ds(order_ref[slot], 1), :]
                picks.append((slot_rows == slots).astype(F32).astype(BF16))
            both = jnp.dot(
                table_ref[...], jnp.concatenate(picks, axis=1), preferred_element_type=F32
            ).astype(BF16)
            for i in range(2):
                left = both[:, i * per_shot : (i + 1) * per_shot]
                target[first + i, :, :per_shot] = left
                target[first + i, :, per_shot:] = jnp.concatenate(
                    [left[64:128], -left[:64], left[192:], -left[128:192]], axis=0
                )

    build(factor_ref, 0)
    build(mine_ref, shots // 2)
    small[3].wait()
    weight_ref[:rays, :half] = ray_ref[:, :half]
    weight_ref[:rays, half:] = -ray_ref[:, half:]
    weight_ref[rays:, :half] = ray_ref[:, half:]
    weight_ref[rays:, half:] = ray_ref[:, :half]

    keep = lambda slot: pltpu.make_async_copy(
        buffer.at[order_ref[shots // 2 + slot]], kept_ref.at[slot], kept_sems.at[slot]
    )

    def wait(first, count):
        for slot in range(first, first + count):
            load(order_ref[slot]).wait()
        if first:
            for slot in range(shots // 2):
                load(order_ref[shots // 2 + slot]).wait()
                keep(slot).start()

    accumulate(
        (4, 4), 0, window_ref, order_ref, lambda slot: buffer[order_ref[slot]], weight_ref,
        factor_ref, high_ref, low_ref, acc_ref, wait,
    )
    put_sums(acc_ref, out_ref)
    for slot in range(shots // 2):
        keep(slot).wait()


def mine_kernel(
    window_hbm, kept_ref, weight_ref, factor_ref, out_ref, window_ref, order_ref, high_ref,
    low_ref, acc_ref, sem,
):
    copy = pltpu.make_async_copy(window_hbm, window_ref, sem)
    copy.start()
    acc_ref[...] = jnp.zeros_like(acc_ref)
    _, core = beam_position()


    def ready():
        copy.wait()
        order_shots(window_ref, order_ref, core)

    accumulate(
        (4, 4), 8, window_ref, order_ref, lambda slot: kept_ref[slot], weight_ref, factor_ref,
        high_ref, low_ref, acc_ref, lambda first, count: None, ready,
    )
    put_sums(acc_ref, out_ref)


def stack(*operands):
    operands = [pltpu.with_memory_space_constraint(jnp.asarray(x), pltpu.HBM) for x in operands]
    window, slots, table, ray_phase, traces = operands
    shots, per_shot, doubled = traces.shape
    rays = ray_phase.shape[0]
    value = pltpu.VMEM((shots // 2 * per_shot, 2 * rays), BF16)
    scalars = pltpu.SMEM(window.shape, jnp.int32)
    acc = pltpu.VMEM((8, 2 * P_SIZE, rays), F32)
    shape = jax.ShapeDtypeStruct
    factor = shape((shots // 2, 256, 2 * per_shot), BF16)
    other, kept, weight, factor = pl.pallas_call(
        other_kernel,
        out_shape=(
            shape((32, 2, 16, rays), BF16),
            shape((shots // 2, per_shot, doubled), BF16),
            shape((2 * rays, doubled), BF16),
            factor,
        ),
        in_specs=[HBM] * 5,
        out_specs=(VMEM,) * 4,
        scratch_shapes=[
            pltpu.VMEM(traces.shape, BF16),
            scalars,
            scalars,
            pltpu.VMEM(slots.shape, jnp.int32),
            pltpu.VMEM(table.shape, BF16),
            pltpu.VMEM(ray_phase.shape, BF16),
            pltpu.VMEM(factor.shape, BF16),
            value,
            value,
            acc,
            pltpu.SemaphoreType.DMA((4,)),
            pltpu.SemaphoreType.DMA((shots,)),
            pltpu.SemaphoreType.DMA((shots // 2,)),
        ],
        compiler_params=pltpu.CompilerParams(vmem_limit_bytes=STACK_VMEM),
        name="stack_other",
    )(*operands)
    mine = lambda: pl.pallas_call(
        mine_kernel,
        out_shape=shape((32, 2, 16, rays), F32),
        in_specs=[HBM, VMEM, VMEM, VMEM],
        out_specs=VMEM,
        scratch_shapes=[scalars, scalars, value, value, acc, pltpu.SemaphoreType.DMA],
        compiler_params=pltpu.CompilerParams(vmem_limit_bytes=MINE_VMEM),
        cost_estimate=pl.CostEstimate(flops=2 << 30, bytes_accessed=8 << 20, transcendentals=0),
        name="stack_mine",
    )(window, kept, weight, factor)
    return other, mine


FIRST_SUM = (20, 1)
FIRST_SPREAD = 21
STACK_VMEM = 32 << 20
MINE_VMEM = 24 << 20
IMAGE_VMEM = 12 << 20


def spread_kernel(arrived_ref, out_ref):
    total = jnp.sum(arrived_ref[...].astype(F32), axis=0).astype(out_ref.dtype)
    for i in range(out_ref.shape[0]):
        out_ref[i] = total


def spread(arrived):
    return pl.pallas_call(
        spread_kernel,
        out_shape=jax.ShapeDtypeStruct((32,) + arrived.shape[1:], BF16),
        in_specs=[VMEM],
        out_specs=VMEM,
        compiler_params=pltpu.CompilerParams(vmem_limit_bytes=8 << 20),
        name="spread",
    )(arrived)


def select(index_ref, table_ref, lane_ref):
    rays = table_ref.shape[-1]
    depths = index_ref.shape[1]
    lane_ref[:WIN_OWN, :depths] = index_ref[...]
    spread_out = lane_ref[...]
    lane = lax.broadcasted_iota(jnp.int32, (1, 128), 1)
    index = jnp.zeros((1, 128), jnp.int32)
    for wl in range(WIN_OWN):
        moved = pltpu.roll(spread_out, wl * depths, 1)[wl : wl + 1]
        here = (lane >= wl * depths) & (lane < (wl + 1) * depths)
        index = jnp.where(here, moved, index)
    rows = lax.broadcasted_iota(jnp.int32, (rays, 128), 0)
    pick = jnp.transpose((rows == index).astype(F32)).astype(BF16)
    group = lax.broadcasted_iota(jnp.int32, (depths, 512), 1) // P_SIZE % WIN_OWN
    table = jnp.concatenate([table_ref[i ^ FIRST_SPREAD] for i in range(32)], axis=0)
    waves = lax.dot_general(pick, table, NT, preferred_element_type=F32)
    wave = waves[:depths]
    for wl in range(1, WIN_OWN):
        wave = jnp.where(group == wl, waves[wl * depths : (wl + 1) * depths], wave)
    return wave.astype(BF16)


def multiply(far, other, wave, basis_ref, out_ref):
    side, core = beam_position()
    chunk = (1 - side if far else side) * 2 + (1 - core if other else core)
    laterals = out_ref.shape[1]
    width = 512
    for i in range(laterals // width):
        columns = pl.ds(pl.multiple_of(chunk * laterals + i * width, width), width)
        basis = basis_ref[:, :, columns].reshape(512, width)
        out_ref[:, i * width : (i + 1) * width] = jnp.dot(
            wave, basis, preferred_element_type=F32
        )


def first_kernel(index_ref, table_ref, basis_ref, out_ref, wave_ref, lane_ref):
    wave_ref[...] = select(index_ref, table_ref, lane_ref)
    multiply(True, True, wave_ref[...], basis_ref, out_ref)


def later_kernel(far, other, wave_ref, basis_ref, out_ref):
    multiply(far, other, wave_ref[...], basis_ref, out_ref)


def image_call(kernel, depths, laterals, basis, wave_out, *operands):
    shape = jax.ShapeDtypeStruct((depths, laterals), F32)
    wave = jax.ShapeDtypeStruct((depths, 512), BF16)
    return pl.pallas_call(
        kernel,
        out_shape=(shape, wave) if wave_out else shape,
        in_specs=[VMEM] * (len(operands) + 1),
        out_specs=(VMEM, VMEM) if wave_out else VMEM,
        scratch_shapes=[pltpu.VMEM((8, 128), jnp.int32)] * wave_out,
        compiler_params=pltpu.CompilerParams(vmem_limit_bytes=IMAGE_VMEM),
        cost_estimate=pl.CostEstimate(
            flops=2 * depths * 512 * laterals, bytes_accessed=1024 * laterals, transcendentals=0
        ),
    )(*operands, basis)


def body(traces, shot_window, trace_slot, ray_phase, ray_index, beam_basis):
    shots, per_shot, _ = traces.shape
    rays = ray_phase.shape[0]
    depths = ray_index.shape[1]
    slabs, beams = lax.axis_size("slab"), lax.axis_size("beam")
    devices = slabs * beams
    chunk = beam_basis.shape[2] // beams
    scale = (shots * devices * per_shot / (WIN_OWN * beams)) ** -0.5
    partner = [(i, i ^ 1) for i in range(devices)]
    distant = [(i, i ^ 2) for i in range(devices)]
    first = FIRST_SUM[0] * 2 + FIRST_SUM[1]
    same_core = [[(i ^ first) * 2 + core for i in range(devices // 2)] for core in range(2)]
    same_beam = [[(i ^ FIRST_SPREAD) * beams + beam for i in range(slabs)] for beam in range(beams)]

    other, mine = stack(shot_window, trace_slot, slant_table(scale), ray_phase, traces)
    other = lax.ppermute(other, AXES, partner)
    both = (mine() + other.astype(F32)).astype(BF16).reshape(2 * slabs, 16, rays)
    arrived = lax.all_to_all(both, AXES, 0, 0, axis_index_groups=same_core, tiled=True)
    table = lax.all_to_all(
        spread(arrived), AXES, 0, 0, axis_index_groups=same_beam, tiled=True
    )

    far_other, wave = image_call(first_kernel, depths, chunk, beam_basis, True, ray_index, table)
    call = lambda far, other, wave: image_call(
        functools.partial(later_kernel, far, other), depths, chunk, beam_basis, False, wave
    )
    far_other = lax.ppermute(far_other, AXES, partner)
    far_mine = call(True, False, wave)
    far = (far_mine + far_other).astype(BF16)
    far = lax.ppermute(far, AXES, distant)
    near_other = call(False, True, wave)
    near_other = lax.ppermute(near_other, AXES, partner)
    near_mine = call(False, False, wave)
    near = lax.optimization_barrier(near_mine + near_other)
    return near + far.astype(F32)


def solution(mesh):
    in_specs = (
        P(("slab", "beam"), None, None),
        P(("slab", "beam")),
        P(("slab", "beam"), None),
        P(),
        P("beam", "slab"),
        P(None, "beam", None),
    )
    return jax.shard_map(
        body, mesh=mesh, in_specs=in_specs, out_specs=P("slab", "beam"), check_vma=False
    )
```
